32 devices in a mesh: rep: 4 (over y, x), tp: 8 (over z, core).
Axes of the slice: x: 2, y: 2, z: 4, core: 2. Of those that a mesh axis runs over, the one named last changes fastest.
Arguments:
- inputs: bfloat16 [2, 2048, 8192], P(None, 'rep', 'tp'), may hold values from -6 to 6
- targets: bfloat16 [2, 2048, 2048], P(None, 'rep', 'tp'), may hold values from -6 to 6
- weight: bfloat16 [8192, 2048], P('tp'), may hold values from -0.0625 to 0.0625
- momentum: float32 [4, 8192, 2048], P('rep', 'tp'), may hold values from -0.8 to 0.8
- indices: int32 [2, 4, 64, 16, 2], P(None, None, 'tp'), may hold values from 0 to 127, as said below
Outputs:
- new_weight: bfloat16 [8192, 2048], P('tp')
- new_momentum: float32 [4, 8192, 2048], P('rep', 'tp')
The draws below stay inside these ranges and needn't reach their ends.
Inputs may be any that keep to these rules, and one draw needn't show every extreme that they name: `indices`: the 2 entries of each block's list are distinct rows of the block's transform.
All inputs are finite; a program needn't handle non-finite values.
Results may differ from the reference program's by a relative error of at most 0.0085.
Values may be sent and summed in bfloat16 or wider, within the bound.
No kernel may reach another device: no remote copies, remote signals or barrier semaphores. Data moves between devices by JAX's collectives and lax.ppermute only.
A program may use at most 128 MiB of HBM per device.

```python
import jax
import jax.numpy as jnp
from jax import lax

DIN = 8192
DOUT = 2048
BLOCK = 128
STEPS = 2
TOK_DEV = 512
TOKENS = 2048
N_REP = 4


def draw_indices(key, part):
    shape = (STEPS, N_REP, DIN // BLOCK, DOUT // BLOCK)
    first_key, second_key = jax.random.split(jax.random.fold_in(key, 11))
    first = jax.random.randint(first_key, shape, 0, BLOCK)
    offset = jax.random.randint(second_key, shape, 1, BLOCK)
    second = (first + offset) % BLOCK
    anchor = jnp.zeros(shape, jnp.int32).at[0, 0, 0, 0].set(1) == 1
    first = jnp.where(anchor, BLOCK - 1, first)
    second = jnp.where(anchor, 0, second)
    return jnp.stack([first, second], axis=-1).astype(jnp.int32)


def levels(stream_key, dims, pieces, least, high):
    def one(axis_at, shards_of):
        heights = jax.random.uniform(jax.random.fold_in(jax.random.fold_in(stream_key, 6), axis_at), (shards_of,), jnp.float32, least / len(pieces), high / len(pieces))
        return jnp.repeat(jnp.exp(heights), dims[axis_at] // shards_of).reshape((-1,) + (1,) * (len(dims) - axis_at - 1))

    level = one(*pieces[0])
    for cut in pieces[1:]:
        level = level * one(*cut)
    return level


def gaussian(key, shape, deviation, reach, pieces=(), held_as=jnp.bfloat16):
    gain = levels(key, shape, pieces, -0.22, 0.18) if pieces else 1.0
    drawn = jax.random.normal(key, shape, jnp.float32) * deviation * gain
    return jnp.minimum(jnp.maximum(drawn, -reach), reach).astype(held_as)


def setup_inputs(seed: int = 0) -> dict:
    streams_of = jax.random.split(jax.random.key(seed), 6)
    return {
        "inputs": gaussian(streams_of[0], (STEPS, TOKENS, DIN), 1.0, 6.0, ((1, 4), (2, 8))),
        "targets": gaussian(streams_of[1], (STEPS, TOKENS, DOUT), 1.0, 6.0, ((1, 4), (2, 8))),
        "weight": gaussian(streams_of[2], (DIN, DOUT), DIN ** -0.5, 0.0625, ((0, 8),)),
        "momentum": gaussian(streams_of[3], (N_REP, DIN, DOUT), 0.1, 0.8, ((0, 4), (1, 8)), jnp.float32),
        "indices": draw_indices(jax.random.fold_in(streams_of[5], 71), 0),
    }


def dct_table(size):
    rows = jnp.arange(size, dtype=jnp.float32)[:, None]
    cols = jnp.arange(size, dtype=jnp.float32)[None, :]
    scale = jnp.where(rows == 0, jnp.sqrt(1.0 / size), jnp.sqrt(2.0 / size))
    return (scale * jnp.cos(jnp.pi * (2.0 * cols + 1.0) * rows / (2.0 * size))).astype(jnp.float32)

def compress(moment, chosen, basis):
    high = lax.Precision.HIGHEST
    blocks = moment.reshape(DIN // BLOCK, BLOCK, DOUT // BLOCK, BLOCK)
    picks = (chosen[..., None] == jnp.arange(BLOCK, dtype=jnp.int32)).astype(jnp.float32)
    rows_sel = jnp.einsum('abjk,kn->abjn', picks, basis, precision=high)
    inner = jnp.einsum('abjn,anbm->abjm', rows_sel, blocks, precision=high)
    coeffs = jnp.einsum('abjm,cm->abjc', inner, basis, precision=high)
    back = jnp.einsum('abjc,cm->abjm', coeffs, basis, precision=high)
    decoded = jnp.einsum('abjn,abjm->anbm', rows_sel, back, precision=high).reshape(DIN, DOUT)
    return (moment - decoded, decoded)

def reference(inputs, targets, weight, momentum, indices):
    basis = dct_table(BLOCK)
    weight_now = weight
    moments = momentum
    for step in range(STEPS):
        acts = inputs[step].reshape(N_REP, TOK_DEV, DIN)
        goals = targets[step].reshape(N_REP, TOK_DEV, DOUT)

        def replica(total, items):
            acts_r, goals_r, moment, chosen = items
            out = jnp.dot(acts_r, weight_now, preferred_element_type=jnp.float32)
            errors = (out - goals_r.astype(jnp.float32)).astype(jnp.bfloat16)
            grad = lax.dot_general(acts_r, errors, (((0,), (0,)), ((), ())), preferred_element_type=jnp.float32) / TOK_DEV
            kept, decoded = compress(0.9 * moment + grad, chosen, basis)
            return (total + decoded, kept)
        update, moments = lax.scan(replica, jnp.zeros((DIN, DOUT), jnp.float32), (acts, goals, moments, indices[step]))
        weight_now = (weight_now.astype(jnp.float32) - 0.1 * update).astype(jnp.bfloat16)
    return (weight_now, moments)
```

```python
import functools

import jax
import jax.numpy as jnp
import numpy as np
from jax import lax
from jax.experimental import pallas as pl
from jax.experimental.pallas import tpu as pltpu
from jax.sharding import PartitionSpec as P

BLOCK = 128
STEPS = 2
CORES = 2
TILE = 256
BF = jnp.bfloat16
F32 = jnp.float32


def dct_table(size):
    rows = np.arange(size, dtype=np.float64)[:, None]
    cols = np.arange(size, dtype=np.float64)[None, :]
    scale = np.where(rows == 0, np.sqrt(1.0 / size), np.sqrt(2.0 / size))
    return (scale * np.cos(np.pi * (2.0 * cols + 1.0) * rows / (2.0 * size))).astype(np.float32)


def parity(value):
    return bin(value).count("1") & 1


def swap_plan(chips, group):
    count = chips.bit_length() - 1
    masks = [1, 3] + [1 << bit for bit in range(2, count)]
    masks = masks[:count]
    if group % 2 and count > 1:
        masks[0], masks[1] = masks[1], masks[0]
    duals = []
    for at in range(count):
        want = [int(at == other) for other in range(count)]
        duals.append(
            next(v for v in range(chips) if [parity(v & mask) for mask in masks] == want)
        )
    return masks, duals


def bit_of(index, functional):
    total = jnp.int32(0)
    for bit in range(functional.bit_length()):
        if functional >> bit & 1:
            total = total ^ (index >> bit & 1)
    return total == 1


def swap(value, axis, size, mask):
    return lax.ppermute(value, axis, [(at, at ^ mask) for at in range(size)])


def dot(left, right):
    return lax.dot_general(left, right, (((1,), (0,)), ((), ())), preferred_element_type=F32)


def cost(flops, moved):
    return pl.CostEstimate(flops=int(flops), bytes_accessed=int(moved), transcendentals=0)


def prep_kernel(all_ref, own_ref, cols_ref, rows_ref, dec_ref, own_dec_ref, kept_ref):
    wide = cols_ref.shape[1]

    def one_hot(picks):
        at = lax.broadcasted_iota(jnp.int32, (wide, picks.shape[-1]), 0)
        return (at == picks).astype(F32).astype(BF)

    for a in range(all_ref.shape[1]):
        dec_ref[0, a] = dot(cols_ref[...], one_hot(all_ref[0, a : a + 1, :])).astype(BF)
        own = one_hot(own_ref[0, a : a + 1, :])
        own_dec_ref[0, a] = dot(cols_ref[...], own).astype(BF)
        part = own.shape[1] // 3 * 2
        kept_ref[0, a] = lax.dot_general(
            own[:, :part],
            rows_ref[...],
            (((0,), (0,)), ((), ())),
            preferred_element_type=F32,
        ).astype(BF)


def prep(picks_all, picks_own):
    count, nbr, width = picks_all.shape
    own = picks_own.shape[2]
    table = dct_table(BLOCK)
    high = np.asarray(table.astype(BF))
    low = np.asarray((table - high.astype(np.float32)).astype(BF))
    rows = np.concatenate([high, low], axis=0)
    cols = np.ascontiguousarray(rows.T)
    part = own // 3 * 2
    spec = lambda shape: pl.BlockSpec((1,) + shape, lambda q: (q,) + (0,) * len(shape))
    whole = lambda shape: pl.BlockSpec(shape, lambda q: (0,) * len(shape))
    return pl.pallas_call(
        prep_kernel,
        grid=(count,),
        in_specs=[spec((nbr, width)), spec((nbr, own)), whole(cols.shape), whole(rows.shape)],
        out_specs=[spec((nbr, BLOCK, width)), spec((nbr, BLOCK, own)), spec((nbr, part, BLOCK))],
        out_shape=[
            jax.ShapeDtypeStruct((count, nbr, BLOCK, width), BF),
            jax.ShapeDtypeStruct((count, nbr, BLOCK, own), BF),
            jax.ShapeDtypeStruct((count, nbr, part, BLOCK), BF),
        ],
        cost_estimate=cost(2 * count * nbr * 256 * 128 * (width + 2 * own), 4 << 20),
        name="prep",
    )(picks_all, picks_own, jnp.asarray(cols), jnp.asarray(rows))


def block_mask(rows, block):
    return lax.broadcasted_iota(jnp.int32, (rows, BLOCK), 0) // 2 == block


def forward_kernel(update, product, slots, *refs):
    refs = list(refs)
    pos = refs.pop(0)
    tile_at = pl.program_id(0)
    w_ref = refs.pop(0)
    if update:
        dec_ref, coef_ref = refs.pop(0), refs.pop(0)
    if product:
        x_ref, t_ref = refs.pop(0), refs.pop(0)
    if update:
        if not product and len(refs) == 2:
            refs.pop(0)
        new_ref = refs.pop(0)
        nbr = dec_ref.shape[1]
        reps = coef_ref.shape[0]
        rows = coef_ref.shape[1] // nbr
        blocks = w_ref.shape[1] // BLOCK
        for a in range(nbr):
            parts = []
            for rep in range(reps):
                coef = coef_ref[rep, a * rows : (a + 1) * rows, :].astype(F32)
                wide = jnp.concatenate(
                    [
                        jnp.where(block_mask(rows, tile_at * blocks + q), coef, 0.0)
                        for q in range(blocks)
                    ],
                    axis=1,
                )
                parts += [wide, wide]
            change = dot(dec_ref[0, a], jnp.concatenate(parts, axis=0).astype(BF))
            span = slice(a * BLOCK, (a + 1) * BLOCK)
            new_ref[span, :] = (w_ref[span, :].astype(F32) - 0.1 * change).astype(BF)
        weight = new_ref
    else:
        weight = w_ref
    if product:
        out_ref = refs.pop(0)
        part = dot(x_ref[0], weight[...])
        blocks = part.shape[1] // BLOCK
        held = t_ref.shape[2] // BLOCK
        out_ref[...] = part.astype(BF)
        for q in range(blocks):
            at = (pos[0] + tile_at) * blocks + q

            @pl.when(at // held == pos[1])
            def _():
                goal = t_ref[0, :, pl.ds(pl.multiple_of(at % held * BLOCK, BLOCK), BLOCK)]
                out_ref[:, q * BLOCK : (q + 1) * BLOCK] = (
                    part[:, q * BLOCK : (q + 1) * BLOCK] - goal.astype(F32)
                ).astype(BF)


def forward(pos, weight, acts, goals, step, width, basis=None, coefs=None, slot=0, half=0, local_w=False):
    rows = weight.shape[0]
    tokens = acts.shape[1]
    tiles = width // TILE
    if local_w:
        w_spec = pl.BlockSpec((rows, TILE), lambda j, p: (0, j))
    else:
        w_spec = pl.BlockSpec((rows, TILE), lambda j, p: (0, p[0] + j))
    in_specs, args = [w_spec], [weight]
    out_specs, out_shape = [], []
    update = basis is not None
    if update:
        in_specs += [
            pl.BlockSpec((1,) + basis.shape[1:], lambda j, p: (slot, 0, 0, 0)),
            pl.BlockSpec((coefs.shape[0], coefs.shape[1] // 2, BLOCK), lambda j, p: (0, half, 0)),
        ]
        args += [basis, coefs]
        out_specs.append(pl.BlockSpec((rows, TILE), lambda j, p: (0, j)))
        out_shape.append(jax.ShapeDtypeStruct((rows, width), BF))
    in_specs += [
        pl.BlockSpec((1, tokens, rows), lambda j, p: (step, 0, 0)),
        pl.BlockSpec((1,) + goals.shape[1:], lambda j, p: (step, 0, 0)),
    ]
    args += [acts, goals]
    out_specs.append(pl.BlockSpec((tokens, TILE), lambda j, p: (0, j)))
    out_shape.append(jax.ShapeDtypeStruct((tokens, width), BF))
    return pl.pallas_call(
        functools.partial(forward_kernel, update, True, None),
        grid_spec=pltpu.PrefetchScalarGridSpec(
            num_scalar_prefetch=1, grid=(tiles,), in_specs=in_specs, out_specs=out_specs
        ),
        out_shape=out_shape,
        cost_estimate=cost(2 * tokens * rows * width, 2 * rows * width * 2),
        name=f"forward{step}",
    )(pos, *args)


def finish_weight(pos, weight, basis, coefs, slot, half, total, previous):
    rows, width = weight.shape
    tiles = width // TILE
    in_specs = [
        pl.BlockSpec((rows, TILE), lambda j, p: (0, j)),
        pl.BlockSpec((1,) + basis.shape[1:], lambda j, p: (slot, 0, 0, 0)),
        pl.BlockSpec((coefs.shape[0], coefs.shape[1] // 2, BLOCK), lambda j, p: (0, half, 0)),
    ]
    args = [weight, basis, coefs]
    alias = {}
    if previous is not None:
        in_specs.append(pl.BlockSpec(memory_space=pl.ANY))
        args.append(previous)
        alias = {4: 0}
    return pl.pallas_call(
        functools.partial(forward_kernel, True, False, None),
        grid_spec=pltpu.PrefetchScalarGridSpec(
            num_scalar_prefetch=1,
            grid=(tiles,),
            in_specs=in_specs,
            out_specs=[pl.BlockSpec((rows, TILE), lambda j, p: (0, p[0] + j))],
        ),
        out_shape=[jax.ShapeDtypeStruct((rows, total), BF)],
        input_output_aliases=alias,
        cost_estimate=cost(2 * rows * 256 * width, 2 * rows * width * 2),
        name="finish",
    )(pos, *args)[0]


def backward_kernel(scale, pos, xt_ref, e_ref, m_ref, kept_ref, dec_ref, *refs):
    refs = list(refs)
    if len(refs) == 4:
        refs.pop(0)
    new_ref, coef_ref, sum_ref = refs
    tile_at = pl.program_id(0)
    nbr = kept_ref.shape[1]
    rows = kept_ref.shape[2] // 2
    moment = m_ref[0] if len(m_ref.shape) == 3 else m_ref[...]
    lead = (0,) if len(new_ref.shape) == 3 else ()
    new_ref[lead + (slice(None), slice(None))] = 0.9 * moment + dot(xt_ref[...], e_ref[...]) * scale
    blocks = TILE // BLOCK
    for a in range(nbr):
        span = lead + (slice(a * BLOCK, (a + 1) * BLOCK), slice(None))
        block = new_ref[span]
        raw = dot(kept_ref[0, a], block.astype(BF))
        coef = raw[:rows] + raw[rows:]
        pieces = [
            jnp.where(
                block_mask(rows, tile_at * blocks + q), coef[:, q * BLOCK : (q + 1) * BLOCK], 0.0
            )
            for q in range(blocks)
        ]
        wide = jnp.concatenate(pieces, axis=1)
        high = wide.astype(BF).astype(F32)
        back = jnp.concatenate([high, high, wide - high], axis=0).astype(BF)
        new_ref[span] = block - dot(dec_ref[0, a], back)
        own = functools.reduce(jnp.add, pieces)
        at = slice(a * rows, (a + 1) * rows)

        @pl.when(tile_at == 0)
        def _():
            sum_ref[at, :] = own

        @pl.when(tile_at > 0)
        def _():
            sum_ref[at, :] += own

    @pl.when(tile_at == pl.num_programs(0) - 1)
    def _():
        coef_ref[...] = sum_ref[...].astype(BF)


def backward(pos, acts_t, errors, moment, kept, own_dec, slot, total=None, previous=None):
    rows, tokens = acts_t.shape
    width = errors.shape[1]
    tiles = width // TILE
    if moment.ndim == 3:
        m_spec = pl.BlockSpec((1, rows, TILE), lambda j, p: (0, 0, p[0] + j))
    else:
        m_spec = pl.BlockSpec((rows, TILE), lambda j, p: (0, j))
    in_specs = [
        pl.BlockSpec((rows, tokens), lambda j, p: (0, 0)),
        pl.BlockSpec((tokens, TILE), lambda j, p: (0, j)),
        m_spec,
        pl.BlockSpec((1,) + kept.shape[1:], lambda j, p: (slot, 0, 0, 0)),
        pl.BlockSpec((1,) + own_dec.shape[1:], lambda j, p: (slot, 0, 0, 0)),
    ]
    args = [acts_t, errors, moment, kept, own_dec]
    alias = {}
    if total is None:
        new_spec = pl.BlockSpec((rows, TILE), lambda j, p: (0, j))
        new_shape = jax.ShapeDtypeStruct((rows, width), F32)
    else:
        new_spec = pl.BlockSpec((1, rows, TILE), lambda j, p: (0, 0, p[0] + j))
        new_shape = jax.ShapeDtypeStruct((1, rows, total), F32)
        if previous is not None:
            in_specs.append(pl.BlockSpec(memory_space=pl.ANY))
            args.append(previous)
            alias = {6: 0}
    coefs = kept.shape[1] * kept.shape[2] // 2
    return pl.pallas_call(
        functools.partial(backward_kernel, 1.0 / tokens),
        grid_spec=pltpu.PrefetchScalarGridSpec(
            num_scalar_prefetch=1,
            grid=(tiles,),
            in_specs=in_specs,
            out_specs=[new_spec, pl.BlockSpec((coefs, BLOCK), lambda j, p: (0, 0))],
            scratch_shapes=[pltpu.VMEM((coefs, BLOCK), F32)],
        ),
        out_shape=[new_shape, jax.ShapeDtypeStruct((coefs, BLOCK), BF)],
        input_output_aliases=alias,
        cost_estimate=cost(2 * rows * tokens * width * 1.6, 2 * rows * width * 4),
        name="backward",
    )(pos, *args)


def flip_if(value, flag, axis):
    return jnp.where(flag, jnp.flip(value, axis), value)


def local(reps, parts, inputs, targets, weight, momentum, indices):
    tokens = inputs.shape[1]
    rows, cols = weight.shape
    nbr, nbc = rows // BLOCK, cols // BLOCK
    chips = parts // CORES
    groups = nbc // parts
    half_blocks = parts // 2
    width = half_blocks * BLOCK
    tiles = width // TILE
    replica = lax.axis_index("rep").astype(jnp.int32)
    place = lax.axis_index("tp").astype(jnp.int32)
    core, chip = place % CORES, place // CORES

    picks = indices.reshape(STEPS, reps, nbr, groups, 2, half_blocks, 2)
    picks = flip_if(picks, core == 1, 4)
    bits = reps.bit_length() - 1
    picks = picks.reshape((STEPS,) + (2,) * bits + picks.shape[2:])
    for bit in range(bits):
        picks = flip_if(picks, (replica >> bit & 1) == 1, bits - bit)
    picks = picks.reshape((STEPS, reps, nbr, groups, 2, half_blocks * 2))
    picks = picks.transpose(0, 3, 4, 2, 1, 5)
    both = jnp.stack([picks, picks + BLOCK], axis=5)
    slots = STEPS * groups * 2
    picks_all = both.reshape(slots, nbr, reps * 2 * half_blocks * 2)
    own = both[..., 0, :, :]
    picks_own = jnp.concatenate([own, own[..., :1, :]], axis=-2).reshape(slots, nbr, -1)
    decode, own_decode, kept = prep(picks_all, picks_own)
    acts_t = [inputs[step].T for step in range(STEPS)]

    def quarter(group, half):
        side = core if half == 0 else 1 - core
        return jnp.stack([(group * 2 + side) * tiles, place])

    slot_of = lambda step, group, half: (step * groups + group) * 2 + half
    weights = [[None, None] for _ in range(groups)]
    moments = [[None, None] for _ in range(groups)]
    coefs = [None] * groups
    final_m = final_w = None
    for step in range(STEPS):
        last = step == STEPS - 1
        partial = [[None, None] for _ in range(groups)]
        for group in range(groups):
            for half in (1, 0):
                pos = quarter(group, half)
                if step == 0:
                    (partial[group][half],) = forward(pos, weight, inputs, targets, step, width)
                else:
                    before = weights[group][half]
                    weights[group][half], partial[group][half] = forward(
                        pos,
                        weight if before is None else before,
                        inputs,
                        targets,
                        step,
                        width,
                        decode,
                        coefs[group],
                        slot_of(step - 1, group, half),
                        half,
                        before is not None,
                    )
        for group in range(groups):
            masks, duals = swap_plan(chips, group)
            total = partial[group][0].astype(F32) + swap(
                partial[group][1], "tp", parts, 1
            ).astype(F32)
            for mask, dual in zip(masks, duals):
                flag = bit_of(chip, dual)
                middle = total.shape[1] // 2
                low, high = total[:, :middle], total[:, middle:]
                sent = jnp.where(flag, low, high).astype(BF)
                total = jnp.where(flag, high, low) + swap(
                    sent, "tp", parts, mask * CORES
                ).astype(F32)
            errors = total.astype(BF)
            for mask, dual in reversed(list(zip(masks, duals))):
                flag = bit_of(chip, dual)
                other = swap(errors, "tp", parts, mask * CORES)
                errors = jnp.concatenate(
                    [jnp.where(flag, other, errors), jnp.where(flag, errors, other)], axis=1
                )
            other = swap(errors, "tp", parts, 1)
            found = []
            for half, err in ((0, errors), (1, other)):
                source = momentum if step == 0 else moments[group][half]
                new, coef = backward(
                    quarter(group, half),
                    acts_t[step],
                    err,
                    source,
                    kept,
                    own_decode,
                    slot_of(step, group, half),
                    cols if last else None,
                    final_m,
                )
                if last:
                    final_m = new
                else:
                    moments[group][half] = new
                found.append(coef)
            gathered = jnp.concatenate(found, axis=0)[None]
            for bit in range(bits):
                gathered = jnp.concatenate(
                    [gathered, swap(gathered, "rep", reps, 1 << bit)], axis=0
                )
            coefs[group] = gathered
    for group in range(groups):
        for half in (0, 1):
            final_w = finish_weight(
                quarter(group, half),
                weights[group][half],
                decode,
                coefs[group],
                slot_of(STEPS - 1, group, half),
                half,
                cols,
                final_w,
            )
    return (final_w, final_m)


def solution(mesh):
    in_specs = (
        P(None, "rep", "tp"),
        P(None, "rep", "tp"),
        P("tp", None),
        P("rep", "tp", None),
        P(None, None, "tp", None, None),
    )
    out_specs = (P("tp", None), P("rep", "tp", None))
    return jax.shard_map(
        functools.partial(local, mesh.shape["rep"], mesh.shape["tp"]),
        mesh=mesh,
        in_specs=in_specs,
        out_specs=out_specs,
        check_vma=False,
    )
```

```python
import functools

import jax
import jax.numpy as jnp
import numpy as np
from jax import lax
from jax.experimental import pallas as pl
from jax.experimental.pallas import tpu as pltpu
from jax.sharding import PartitionSpec as P

BLOCK = 128
STEPS = 2
CORES = 2
BF = jnp.bfloat16
F32 = jnp.float32


def dct_table(size):
    rows = np.arange(size, dtype=np.float64)[:, None]
    cols = np.arange(size, dtype=np.float64)[None, :]
    scale = np.where(rows == 0, np.sqrt(1.0 / size), np.sqrt(2.0 / size))
    return (scale * np.cos(np.pi * (2.0 * cols + 1.0) * rows / (2.0 * size))).astype(np.float32)


def swap(value, axis, size, mask):
    return lax.ppermute(value, axis, [(at, at ^ mask) for at in range(size)])


def dot(left, right):
    return lax.dot_general(left, right, (((1,), (0,)), ((), ())), preferred_element_type=F32)


def room(mib):
    return pltpu.CompilerParams(vmem_limit_bytes=mib << 20)


def cost(flops, moved):
    return pl.CostEstimate(flops=int(flops), bytes_accessed=int(moved), transcendentals=0)


def shaped(shape, dtype):
    return jax.ShapeDtypeStruct(shape, dtype)


def call(kernel, name, grid, ins, outs, mib, work, place, aliased=None):
    alias = {}
    arrays = [array for array, _, _ in ins]
    specs = [pl.BlockSpec(block, index) for _, block, index in ins]
    if aliased is not None:
        arrays.append(aliased)
        specs.append(pl.BlockSpec(memory_space=pl.ANY))
        alias = {len(arrays): 0}
    return pl.pallas_call(
        kernel,
        grid_spec=pltpu.PrefetchScalarGridSpec(
            num_scalar_prefetch=1,
            grid=(grid,),
            in_specs=specs,
            out_specs=[pl.BlockSpec(block, index) for _, block, index in outs],
        ),
        out_shape=[shape for shape, _, _ in outs],
        input_output_aliases=alias,
        compiler_params=room(mib),
        cost_estimate=cost(*work),
        name=name,
    )(place, *arrays)


def row_mask(rows, lanes, per, count, wanted, axis):
    return lax.broadcasted_iota(jnp.int32, (rows, lanes), axis) // per % count == wanted


def spread_rows(kept, nbr, per):
    kept = kept.astype(F32)
    return jnp.concatenate(
        [jnp.where(row_mask(*kept.shape, per, nbr, a, 0), kept, 0.0) for a in range(nbr)], axis=1
    ).astype(BF)


def spread_cols(basis, nbr, per):
    basis = basis.astype(F32)
    return jnp.concatenate(
        [jnp.where(row_mask(*basis.shape, per, nbr, a, 1), basis, 0.0) for a in range(nbr)], axis=0
    ).astype(BF)


def widen(coef, blocks):
    return jnp.concatenate(
        [jnp.where(row_mask(*coef.shape, 2, blocks, q, 0), coef, 0.0) for q in range(blocks)],
        axis=1,
    )


def narrow(wide, blocks):
    rows = wide.shape[0]
    return functools.reduce(
        jnp.add,
        [
            jnp.where(
                row_mask(rows, BLOCK, 2, blocks, q, 0), wide[:, q * BLOCK : (q + 1) * BLOCK], 0.0
            )
            for q in range(blocks)
        ],
    )


def fold(pair):
    half = pair.shape[0] // 2
    return pair[:half] + pair[half:]


def prep_kernel(place, all_ref, own_ref, cols_ref, rows_ref, dec_ref, own_dec_ref, kept_ref):
    wide = cols_ref.shape[1]

    def one_hot(picks):
        at = lax.broadcasted_iota(jnp.int32, (wide, picks.shape[-1]), 0)
        return (at == picks).astype(F32).astype(BF)

    dec_ref[0] = dot(cols_ref[...], one_hot(all_ref[0])).astype(BF)
    own = one_hot(own_ref[0])
    own_dec_ref[0] = dot(cols_ref[...], own).astype(BF)
    part = own.shape[1] // 3 * 2
    kept_ref[0] = lax.dot_general(
        own[:, :part], rows_ref[...], (((0,), (0,)), ((), ())), preferred_element_type=F32
    ).astype(BF)


def prep(place, picks_all, picks_own):
    tiles, _, width = picks_all.shape
    own = picks_own.shape[2]
    part = own // 3 * 2
    table = dct_table(BLOCK)
    high = np.asarray(table.astype(BF))
    low = np.asarray((table - high.astype(np.float32)).astype(BF))
    rows = jnp.asarray(np.concatenate([high, low], axis=0))
    cols = jnp.asarray(np.ascontiguousarray(np.concatenate([high, low], axis=0).T))
    each = lambda q, p: (q, 0, 0)
    once = lambda q, p: (0, 0)
    return call(
        prep_kernel,
        "prep",
        tiles,
        [
            (picks_all, (1, 1, width), each),
            (picks_own, (1, 1, own), each),
            (cols, cols.shape, once),
            (rows, rows.shape, once),
        ],
        [
            (shaped((tiles, BLOCK, width), BF), (1, BLOCK, width), each),
            (shaped((tiles, BLOCK, own), BF), (1, BLOCK, own), each),
            (shaped((tiles, part, BLOCK), BF), (1, part, BLOCK), each),
        ],
        4,
        (2 * tiles * 256 * 128 * (width + 2 * own), 2 << 20),
        place,
    )


def project_kernel(nbr, per, place, kept_ref, xt_ref, out_ref):
    tiles = kept_ref.shape[0]
    left = jnp.concatenate([spread_rows(kept_ref[q], nbr, per) for q in range(tiles)], axis=0)
    both = dot(left, xt_ref[...])
    pair = kept_ref.shape[1]
    for q in range(tiles):
        value = fold(both[q * pair : (q + 1) * pair])
        high = value.astype(BF)
        out_ref[q] = jnp.concatenate(
            [high.astype(F32), value - high.astype(F32)], axis=0
        ).astype(BF)


def project(place, kept, acts_t, nbr, per):
    tiles, pair, _ = kept.shape
    rows, tokens = acts_t.shape
    return call(
        functools.partial(project_kernel, nbr, per),
        "project",
        1,
        [
            (kept, kept.shape, lambda j, p: (0, 0, 0)),
            (acts_t, acts_t.shape, lambda j, p: (0, 0)),
        ],
        [(shaped((tiles, pair, tokens), BF), (tiles, pair, tokens), lambda j, p: (0, 0, 0))],
        12,
        (2 * tiles * pair * rows * tokens, 2 * rows * tokens),
        place,
    )[0]


def keep_rows(kept, moment, nbr, per, blocks):
    return narrow(fold(dot(spread_rows(kept, nbr, per), moment.astype(BF))), blocks)


def moment_rows_kernel(nbr, per, place, kept_ref, m_ref, out_ref):
    out_ref[0] = keep_rows(kept_ref[0], m_ref[0], nbr, per, m_ref.shape[2] // BLOCK)


def moment_rows(place, kept, momentum, tile, per):
    tiles, pair, _ = kept.shape
    rows = momentum.shape[1]
    return call(
        functools.partial(moment_rows_kernel, rows // BLOCK, per),
        "moment_rows",
        tiles,
        [
            (kept, (1, pair, BLOCK), lambda j, p: (j, 0, 0)),
            (momentum, (1, rows, tile), lambda j, p: (0, 0, j ^ p[0])),
        ],
        [(shaped((tiles, pair // 2, BLOCK), F32), (1, pair // 2, BLOCK), lambda j, p: (j, 0, 0))],
        8,
        (2 * tiles * pair * rows * tile, 4 * rows * tile * tiles),
        place,
    )[0]


def coef_kernel(scale, place, proj_ref, e_ref, old_ref, exact_ref, sent_ref):
    blocks = e_ref.shape[2] // BLOCK
    for q in range(proj_ref.shape[0]):
        value = 0.9 * old_ref[q] + scale * narrow(fold(dot(proj_ref[q], e_ref[q])), blocks)
        exact_ref[q] = value
        sent_ref[q] = value.astype(BF)


def coefficients(place, proj, errors, old, chunk):
    tiles, tokens, tile = errors.shape
    pair = proj.shape[1]
    shape = (tiles, pair // 2, BLOCK)
    part = lambda j, p: (chunk, 0, 0)
    whole = lambda j, p: (0, 0, 0)
    return call(
        functools.partial(coef_kernel, 1.0 / tokens),
        "coefficients",
        1,
        [
            (proj, (tiles, pair, tokens), part),
            (errors, errors.shape, whole),
            (old, shape, part),
        ],
        [(shaped(shape, F32), shape, whole), (shaped(shape, BF), shape, whole)],
        8,
        (2 * tiles * pair * tokens * tile, 2 * tiles * tokens * tile),
        place,
    )


def momentum_kernel(scale, nbr, per, follow, place, xt_ref, e_ref, m_ref, dec_ref, coef_ref, *refs):
    refs = list(refs)
    kept_ref = refs.pop(0) if follow else None
    if len(refs) == 2 and not follow:
        refs.pop(0)
    coef = widen(coef_ref[0], m_ref.shape[2] // BLOCK)
    high = coef.astype(BF).astype(F32)
    back = jnp.concatenate([high, high, coef - high], axis=0).astype(BF)
    new = 0.9 * m_ref[0] + (
        dot(xt_ref[...], e_ref[0]) * scale - dot(spread_cols(dec_ref[0], nbr, per), back)
    )
    refs[0][0] = new
    if follow:
        refs[1][0] = keep_rows(kept_ref[0], new, nbr, per, new.shape[1] // BLOCK)


def momentum_step(place, acts_t, errors, moment, own_dec, coef, per, start, kept_next, total, previous):
    rows, tokens = acts_t.shape
    tiles, _, tile = errors.shape
    nbr = rows // BLOCK
    follow = kept_next is not None
    each = lambda j, p: (start + j, 0, 0)
    here = lambda j, p: (j, 0, 0)
    natural = lambda j, p: (0, 0, (start + j) ^ p[0])
    ins = [
        (acts_t, acts_t.shape, lambda j, p: (0, 0)),
        (errors, (1, tokens, tile), here),
        (moment, (1, rows, tile), natural if moment.shape[0] == 1 else each),
        (own_dec, (1,) + own_dec.shape[1:], each),
        (coef, (1,) + coef.shape[1:], here),
    ]
    outs = []
    if follow:
        ins.append((kept_next, (1,) + kept_next.shape[1:], each))
        outs.append((shaped((tiles, rows, tile), F32), (1, rows, tile), here))
        shape = coef.shape
        outs.append((shaped(shape, F32), (1,) + shape[1:], here))
    else:
        outs.append((shaped((1, rows, total), F32), (1, rows, tile), natural))
    return call(
        functools.partial(momentum_kernel, 1.0 / tokens, nbr, per, follow),
        "momentum",
        tiles,
        ins,
        outs,
        14,
        (2 * rows * tokens * tile * tiles, 8 * rows * tile * tiles),
        place,
        previous,
    )


def changed(weight, dec_ref, coef_ref, nbr, per):
    blocks = weight.shape[1] // BLOCK
    parts = []
    for rep in range(coef_ref.shape[0]):
        parts += [widen(coef_ref[rep, 0].astype(F32), blocks)] * 2
    change = dot(spread_cols(dec_ref[0], nbr, per), jnp.concatenate(parts, axis=0).astype(BF))
    return (weight.astype(F32) - 0.1 * change).astype(BF)


def first_kernel(place, w_ref, x_ref, out_ref):
    out_ref[0] = dot(x_ref[0], w_ref[...]).astype(BF)


def next_kernel(nbr, per, place, w_ref, x_ref, dec_ref, coef_ref, new_ref, out_ref):
    new = changed(w_ref[...], dec_ref, coef_ref, nbr, per)
    new_ref[0] = new
    out_ref[0] = dot(x_ref[0], new).astype(BF)


def forward(place, weight, acts, step, tile, per, start, core, count, basis=None, coefs=None):
    rows = weight.shape[0]
    tokens = acts.shape[1]
    at = lambda j: CORES * (start + j) + core
    ins = [
        (weight, (rows, tile), lambda j, p: (0, at(j) ^ p[0])),
        (acts, (1, tokens, rows), lambda j, p: (step, 0, 0)),
    ]
    product = (shaped((count, tokens, tile), BF), (1, tokens, tile), lambda j, p: (j, 0, 0))
    work = (2 * tokens * rows * tile * count, 2 * rows * tile * count + 2 * tokens * rows)
    if basis is None:
        return call(first_kernel, "first", count, ins, [product], 40, work, place)[0]
    ins += [
        (basis, (1,) + basis.shape[1:], lambda j, p: (at(j), 0, 0)),
        (
            coefs,
            (coefs.shape[0], 1) + coefs.shape[2:],
            lambda j, p: (0, CORES * j + core, 0, 0),
        ),
    ]
    new = (shaped((count, rows, tile), BF), (1, rows, tile), lambda j, p: (j, 0, 0))
    return call(
        functools.partial(next_kernel, rows // BLOCK, per),
        "next",
        count,
        ins,
        [new, product],
        12,
        work,
        place,
    )


def finish_kernel(nbr, per, place, keep_ref, send_ref, dec_ref, coef_ref, *refs):
    here = pl.program_id(0) % CORES == 0

    @pl.when(here)
    def _():
        refs[-1][...] = changed(keep_ref[0], dec_ref, coef_ref, nbr, per)

    @pl.when(jnp.logical_not(here))
    def _():
        refs[-1][...] = changed(send_ref[0], dec_ref, coef_ref, nbr, per)


def finish(place, keep, send, basis, coefs, per, start, total, previous):
    count, rows, tile = keep.shape
    each = lambda j, p: (j // CORES, 0, 0)
    return call(
        functools.partial(finish_kernel, rows // BLOCK, per),
        "finish",
        count * CORES,
        [
            (keep, (1, rows, tile), each),
            (send, (1, rows, tile), each),
            (basis, (1,) + basis.shape[1:], lambda j, p: (CORES * start + j, 0, 0)),
            (coefs, (coefs.shape[0], 1) + coefs.shape[2:], lambda j, p: (0, j, 0, 0)),
        ],
        [(shaped((rows, total), BF), (rows, tile), lambda j, p: (0, (CORES * start + j) ^ p[0]))],
        12,
        (2 * rows * 256 * tile * count * CORES, 4 * rows * tile * count * CORES),
        place,
        previous,
    )[0]


def by_distance(value, axes, index):
    for place, axis in enumerate(reversed(axes)):
        value = jnp.where((index >> place & 1) == 1, jnp.flip(value, axis), value)
    return value


def pick_tables(indices, step, reps, parts, replica, tp):
    nbr, nbc = indices.shape[2], indices.shape[3]
    per = nbc // parts * 2
    rep_bits, tp_bits = reps.bit_length() - 1, parts.bit_length() - 1
    picks = indices[step].reshape((2,) * rep_bits + (nbr,) + (2,) * tp_bits + (per,))
    picks = by_distance(picks, range(rep_bits), replica)
    picks = by_distance(picks, range(rep_bits + 1, rep_bits + 1 + tp_bits), tp)
    picks = picks.reshape(reps, nbr, parts, per).transpose(2, 0, 1, 3)
    picks = picks.reshape(parts, reps, nbr * per)
    both = jnp.concatenate([picks, picks + BLOCK], axis=2)
    own = jnp.concatenate([both[:, 0], picks[:, 0]], axis=1)
    return both.reshape(parts, 1, -1), own.reshape(parts, 1, -1), per


def local(reps, parts, inputs, targets, weight, momentum, indices):
    rows, cols = weight.shape
    nbr = rows // BLOCK
    tile = cols // parts
    chips = parts // CORES
    count = chips // 2
    replica = lax.axis_index("rep").astype(jnp.int32)
    tp = lax.axis_index("tp").astype(jnp.int32)
    place = tp[None]
    chunks = (0, 1)

    acts_t, tables = [], []
    for step in range(STEPS):
        picks_all, picks_own, per = pick_tables(indices, step, reps, parts, replica, tp)
        tables.append(prep(place, picks_all, picks_own))
        acts_t.append(inputs[step].T)
    projected = [project(place, tables[s][2], acts_t[s], nbr, per) for s in range(STEPS)]
    old = moment_rows(place, tables[0][2], momentum, tile, per)

    moment = momentum
    gathered = [None, None]
    weights = [[None, None], [None, None]]
    final_m = final_w = None
    for step in range(STEPS):
        last = step == STEPS - 1
        totals = [None] * chips
        for chunk in (1, 0) if step == 0 else (0, 1):
            start = chunk * count
            found = [None, None]
            for core in (1, 0):
                if step == 0:
                    found[core] = forward(
                        place, weight, inputs, step, tile, per, start, core, count
                    )
                else:
                    weights[chunk][core], found[core] = forward(
                        place,
                        weight,
                        inputs,
                        step,
                        tile,
                        per,
                        start,
                        core,
                        count,
                        tables[step - 1][0],
                        gathered[chunk],
                    )
                if core == 1:
                    other = swap(found[1], "tp", parts, 1)
            for at in range(count):
                totals[start + at] = found[0][at].astype(F32) + other[at].astype(F32)
        total = totals[0] - targets[step].astype(F32)
        for mask in range(1, chips):
            total = total + swap(
                totals[mask].astype(BF), "tp", parts, mask * CORES
            ).astype(F32)
        errors = total.astype(BF)
        pieces = [errors] + [
            swap(errors, "tp", parts, mask * CORES) for mask in range(1, chips)
        ]
        stacks, exact = [], []
        for chunk in chunks:
            mine = pieces[chunk * count : (chunk + 1) * count]
            pairs = []
            for piece in mine:
                pairs += [piece, swap(piece, "tp", parts, 1)]
            stack = jnp.stack(pairs)
            value, sent = coefficients(place, projected[step], stack, old, chunk)
            gathered[chunk] = jnp.stack(
                [sent] + [swap(sent, "rep", reps, mask) for mask in range(1, reps)]
            )
            stacks.append(stack)
            exact.append(value)
        if not last:
            moment, old = momentum_step(
                place,
                acts_t[step],
                jnp.concatenate(stacks),
                moment,
                tables[step][1],
                jnp.concatenate(exact),
                per,
                0,
                tables[step + 1][2],
                cols,
                None,
            )
        else:
            for chunk in chunks:
                final_m = momentum_step(
                    place,
                    acts_t[step],
                    stacks[chunk],
                    moment,
                    tables[step][1],
                    exact[chunk],
                    per,
                    chunk * count * CORES,
                    None,
                    cols,
                    final_m,
                )[0]
    for chunk in chunks:
        final_w = finish(
            place,
            weights[chunk][0],
            weights[chunk][1],
            tables[STEPS - 1][0],
            gathered[chunk],
            per,
            chunk * count,
            cols,
            final_w,
        )
    return (final_w, final_m)


def solution(mesh):
    in_specs = (
        P(None, "rep", "tp"),
        P(None, "rep", "tp"),
        P("tp", None),
        P("rep", "tp", None),
        P(None, None, "tp", None, None),
    )
    out_specs = (P("tp", None), P("rep", "tp", None))
    return jax.shard_map(
        functools.partial(local, mesh.shape["rep"], mesh.shape["tp"]),
        mesh=mesh,
        in_specs=in_specs,
        out_specs=out_specs,
        check_vma=False,
    )
```

```python
import functools

import jax
import jax.numpy as jnp
import numpy as np
from jax import lax
from jax.experimental import pallas as pl
from jax.experimental.pallas import tpu as pltpu
from jax.sharding import PartitionSpec as P


BLOCK = 128
STEPS = 2
CORES = 2
BF = jnp.bfloat16
F32 = jnp.float32


def dct_table(size):
    rows = np.arange(size, dtype=np.float64)[:, None]
    cols = np.arange(size, dtype=np.float64)[None, :]
    scale = np.where(rows == 0, np.sqrt(1.0 / size), np.sqrt(2.0 / size))
    return (scale * np.cos(np.pi * (2.0 * cols + 1.0) * rows / (2.0 * size))).astype(np.float32)


def swap(value, axis, size, mask):
    return lax.ppermute(value, axis, [(at, at ^ mask) for at in range(size)])


def dot(left, right):
    return lax.dot_general(left, right, (((1,), (0,)), ((), ())), preferred_element_type=F32)


def room(mib):
    return pltpu.CompilerParams(vmem_limit_bytes=mib << 20)


def cost(flops, moved):
    return pl.CostEstimate(flops=int(flops), bytes_accessed=int(moved), transcendentals=0)


def shaped(shape, dtype):
    return jax.ShapeDtypeStruct(shape, dtype)


def call(kernel, grid, ins, outs, mib, work, place, aliased=None):
    alias = {}
    arrays = [array for array, _, _ in ins]
    specs = [pl.BlockSpec(block, index) for _, block, index in ins]
    if aliased is not None:
        arrays.append(aliased)
        specs.append(pl.BlockSpec(memory_space=pl.ANY))
        alias = {len(arrays): 0}
    return pl.pallas_call(
        kernel,
        grid_spec=pltpu.PrefetchScalarGridSpec(
            num_scalar_prefetch=1,
            grid=(grid,),
            in_specs=specs,
            out_specs=[pl.BlockSpec(block, index) for _, block, index in outs],
        ),
        out_shape=[shape for shape, _, _ in outs],
        input_output_aliases=alias,
        compiler_params=room(mib),
        cost_estimate=cost(*work),
    )(place, *arrays)


def row_mask(rows, lanes, per, count, wanted, axis):
    return lax.broadcasted_iota(jnp.int32, (rows, lanes), axis) // per % count == wanted


def spread_rows(kept, nbr, per):
    kept = kept.astype(F32)
    return jnp.concatenate(
        [jnp.where(row_mask(*kept.shape, per, nbr, a, 0), kept, 0.0) for a in range(nbr)], axis=1
    ).astype(BF)


def spread_cols(basis, nbr, per):
    basis = basis.astype(F32)
    return jnp.concatenate(
        [jnp.where(row_mask(*basis.shape, per, nbr, a, 1), basis, 0.0) for a in range(nbr)], axis=0
    ).astype(BF)


def widen(coef, blocks):
    return jnp.concatenate(
        [jnp.where(row_mask(*coef.shape, 2, blocks, q, 0), coef, 0.0) for q in range(blocks)],
        axis=1,
    )


def narrow(wide, blocks):
    rows = wide.shape[0]
    return functools.reduce(
        jnp.add,
        [
            jnp.where(
                row_mask(rows, BLOCK, 2, blocks, q, 0), wide[:, q * BLOCK : (q + 1) * BLOCK], 0.0
            )
            for q in range(blocks)
        ],
    )


def fold(pair):
    half = pair.shape[0] // 2
    return pair[:half] + pair[half:]


def prep_kernel(place, all_ref, own_ref, cols_ref, rows_ref, dec_ref, own_dec_ref, kept_ref):
    wide = cols_ref.shape[1]

    def one_hot(picks):
        at = lax.broadcasted_iota(jnp.int32, (wide, picks.shape[-1]), 0)
        return (at == picks).astype(F32).astype(BF)

    dec_ref[0] = dot(cols_ref[...], one_hot(all_ref[0])).astype(BF)
    own = one_hot(own_ref[0])
    own_dec_ref[0] = dot(cols_ref[...], own).astype(BF)
    part = own.shape[1] // 3 * 2
    kept_ref[0] = lax.dot_general(
        own[:, :part], rows_ref[...], (((0,), (0,)), ((), ())), preferred_element_type=F32
    ).astype(BF)


def prep(place, picks_all, picks_own):
    tiles, _, width = picks_all.shape
    own = picks_own.shape[2]
    part = own // 3 * 2
    table = dct_table(BLOCK)
    high = np.asarray(table.astype(BF))
    low = np.asarray((table - high.astype(np.float32)).astype(BF))
    rows = jnp.asarray(np.concatenate([high, low], axis=0))
    cols = jnp.asarray(np.ascontiguousarray(np.concatenate([high, low], axis=0).T))
    each = lambda q, p: (q, 0, 0)
    once = lambda q, p: (0, 0)
    return call(
        prep_kernel,
        tiles,
        [
            (picks_all, (1, 1, width), each),
            (picks_own, (1, 1, own), each),
            (cols, cols.shape, once),
            (rows, rows.shape, once),
        ],
        [
            (shaped((tiles, BLOCK, width), BF), (1, BLOCK, width), each),
            (shaped((tiles, BLOCK, own), BF), (1, BLOCK, own), each),
            (shaped((tiles, part, BLOCK), BF), (1, part, BLOCK), each),
        ],
        4,
        (2 * tiles * 256 * 128 * (width + 2 * own), 2 << 20),
        place,
    )


def project_kernel(nbr, per, place, kept_ref, x_ref, out_ref, xt_ref):
    tiles = kept_ref.shape[0]
    xt_ref[...] = x_ref[0].T
    left = jnp.concatenate([spread_rows(kept_ref[q], nbr, per) for q in range(tiles)], axis=0)
    both = dot(left, xt_ref[...])
    pair = kept_ref.shape[1]
    for q in range(tiles):
        value = fold(both[q * pair : (q + 1) * pair])
        high = value.astype(BF)
        out_ref[q] = jnp.concatenate(
            [high.astype(F32), value - high.astype(F32)], axis=0
        ).astype(BF)


def project(place, kept, acts, step, nbr, per):
    tiles, pair, _ = kept.shape
    _, tokens, rows = acts.shape
    return call(
        functools.partial(project_kernel, nbr, per),
        1,
        [
            (kept, kept.shape, lambda j, p: (0, 0, 0)),
            (acts, (1, tokens, rows), lambda j, p: (step, 0, 0)),
        ],
        [
            (shaped((tiles, pair, tokens), BF), (tiles, pair, tokens), lambda j, p: (0, 0, 0)),
            (shaped((rows, tokens), BF), (rows, tokens), lambda j, p: (0, 0)),
        ],
        14,
        (2 * tiles * pair * rows * tokens, 4 * rows * tokens),
        place,
    )


def keep_rows(kept, moment, nbr, per, blocks):
    return narrow(fold(dot(spread_rows(kept, nbr, per), moment.astype(BF))), blocks)


def moment_rows_kernel(nbr, per, place, kept_ref, m_ref, out_ref):
    out_ref[0] = keep_rows(kept_ref[0], m_ref[0], nbr, per, m_ref.shape[2] // BLOCK)


def moment_rows(place, kept, momentum, tile, per):
    tiles, pair, _ = kept.shape
    rows = momentum.shape[1]
    return call(
        functools.partial(moment_rows_kernel, rows // BLOCK, per),
        tiles,
        [
            (kept, (1, pair, BLOCK), lambda j, p: (j, 0, 0)),
            (momentum, (1, rows, tile), lambda j, p: (0, 0, j ^ p[0])),
        ],
        [(shaped((tiles, pair // 2, BLOCK), F32), (1, pair // 2, BLOCK), lambda j, p: (j, 0, 0))],
        8,
        (2 * tiles * pair * rows * tile, 4 * rows * tile * tiles),
        place,
    )[0]


def coef_kernel(scale, place, proj_ref, old_ref, *refs):
    *e_refs, exact_ref, sent_ref = refs
    blocks = e_refs[0].shape[1] // BLOCK
    for q, e_ref in enumerate(e_refs):
        value = 0.9 * old_ref[q] + scale * narrow(fold(dot(proj_ref[q], e_ref[...])), blocks)
        exact_ref[q] = value
        sent_ref[q] = value.astype(BF)


def coefficients(place, proj, errors, old):
    tiles = len(errors)
    tokens, tile = errors[0].shape
    pair = proj.shape[1]
    shape = (tiles, pair // 2, BLOCK)
    whole = lambda j, p: (0, 0, 0)
    return call(
        functools.partial(coef_kernel, 1.0 / tokens),
        1,
        [(proj, (tiles, pair, tokens), whole), (old, shape, whole)]
        + [(piece, piece.shape, lambda j, p: (0, 0)) for piece in errors],
        [(shaped(shape, F32), shape, whole), (shaped(shape, BF), shape, whole)],
        8,
        (2 * tiles * pair * tokens * tile, 2 * tiles * tokens * tile),
        place,
    )


def momentum_kernel(scale, nbr, per, follow, place, xt_ref, e_ref, m_ref, dec_ref, coef_ref, *refs):
    refs = list(refs)
    kept_ref = refs.pop(0) if follow else None
    if len(refs) == 2 and not follow:
        refs.pop(0)
    coef = widen(coef_ref[0], m_ref.shape[2] // BLOCK)
    high = coef.astype(BF).astype(F32)
    back = jnp.concatenate([high, high, coef - high], axis=0).astype(BF)
    new = 0.9 * m_ref[0] + (
        dot(xt_ref[...], e_ref[0]) * scale - dot(spread_cols(dec_ref[0], nbr, per), back)
    )
    refs[0][0] = new
    if follow:
        refs[1][0] = keep_rows(kept_ref[0], new, nbr, per, new.shape[1] // BLOCK)


def momentum_step(place, acts_t, errors, moment, own_dec, coef, per, start, kept_next, total, previous):
    rows, tokens = acts_t.shape
    tiles, _, tile = errors.shape
    nbr = rows // BLOCK
    follow = kept_next is not None
    each = lambda j, p: (start + j, 0, 0)
    here = lambda j, p: (j, 0, 0)
    natural = lambda j, p: (0, 0, (start + j) ^ p[0])
    ins = [
        (acts_t, acts_t.shape, lambda j, p: (0, 0)),
        (errors, (1, tokens, tile), here),
        (moment, (1, rows, tile), natural if moment.shape[0] == 1 else each),
        (own_dec, (1,) + own_dec.shape[1:], each),
        (coef, (1,) + coef.shape[1:], each),
    ]
    outs = []
    if follow:
        ins.append((kept_next, (1,) + kept_next.shape[1:], each))
        outs.append((shaped((tiles, rows, tile), F32), (1, rows, tile), here))
        outs.append((shaped(coef.shape, F32), (1,) + coef.shape[1:], here))
    else:
        outs.append((shaped((1, rows, total), F32), (1, rows, tile), natural))
    return call(
        functools.partial(momentum_kernel, 1.0 / tokens, nbr, per, follow),
        tiles,
        ins,
        outs,
        14,
        (2 * rows * tokens * tile * tiles, 8 * rows * tile * tiles),
        place,
        previous,
    )


def changed(weight, dec_ref, coef_refs, nbr, per):
    blocks = weight.shape[1] // BLOCK
    parts = []
    for coef_ref in coef_refs:
        parts += [widen(coef_ref[0].astype(F32), blocks)] * 2
    change = dot(spread_cols(dec_ref[0], nbr, per), jnp.concatenate(parts, axis=0).astype(BF))
    return (weight.astype(F32) - 0.1 * change).astype(BF)


def first_kernel(start, core, place, w_ref, x_ref, out_ref, w_buf, x_buf, sum_ref, sems):
    count, rows, tile = w_buf.shape
    step = x_buf.shape[2]
    copies = []
    for k in range(rows // step):
        span = slice(k * step, (k + 1) * step)
        copies.append([pltpu.make_async_copy(x_ref.at[0, :, span], x_buf.at[k], sems.at[k, count])])
        for at in range(count):
            column = ((CORES * (start + at) + core) ^ place[0]) * tile
            source = w_ref.at[span, pl.ds(pl.multiple_of(column, tile), tile)]
            target = w_buf.at[at, span, :]
            copies[k].append(pltpu.make_async_copy(source, target, sems.at[k, at]))
    for group in copies:
        for copy in group:
            copy.start()
    for k, group in enumerate(copies):
        group[0].wait()
        for at in range(count):
            group[at + 1].wait()
            part = dot(x_buf[k], w_buf[at, k * step : (k + 1) * step, :])
            if k > 0:
                part = part + sum_ref[at]
            if k < len(copies) - 1:
                sum_ref[at] = part
            else:
                out_ref[at] = part.astype(BF)


def first(place, weight, acts, tile, start, core, count):
    rows = weight.shape[0]
    tokens = acts.shape[1]
    step = 256
    return pl.pallas_call(
        functools.partial(first_kernel, start, core),
        grid_spec=pltpu.PrefetchScalarGridSpec(
            num_scalar_prefetch=1,
            grid=(1,),
            in_specs=[pl.BlockSpec(memory_space=pltpu.HBM)] * 2,
            out_specs=pl.BlockSpec((count, tokens, tile), lambda j, p: (0, 0, 0)),
            scratch_shapes=[
                pltpu.VMEM((count, rows, tile), BF),
                pltpu.VMEM((rows // step, tokens, step), BF),
                pltpu.VMEM((count, tokens, tile), F32),
                pltpu.SemaphoreType.DMA((rows // step, count + 1)),
            ],
        ),
        out_shape=shaped((count, tokens, tile), BF),
        compiler_params=room(52),
        cost_estimate=cost(2 * tokens * rows * tile * count, 2 * rows * (tile * count + tokens)),
        name="first",
    )(place, weight, acts)


def next_kernel(nbr, per, place, w_ref, x_ref, dec_ref, *refs):
    *coef_refs, new_ref, out_ref = refs
    new = changed(w_ref[...], dec_ref, coef_refs, nbr, per)
    new_ref[0] = new
    out_ref[0] = dot(x_ref[0], new).astype(BF)


def forward(place, weight, acts, step, tile, per, start, core, count, basis, coefs):
    rows = weight.shape[0]
    tokens = acts.shape[1]
    at = lambda j: CORES * (start + j) + core
    ins = [
        (weight, (rows, tile), lambda j, p: (0, at(j) ^ p[0])),
        (acts, (1, tokens, rows), lambda j, p: (step, 0, 0)),
        (basis, (1,) + basis.shape[1:], lambda j, p: (at(j), 0, 0)),
    ]
    for coef in coefs:
        ins.append((coef, (1,) + coef.shape[1:], lambda j, p: (at(j), 0, 0)))
    product = (shaped((count, tokens, tile), BF), (1, tokens, tile), lambda j, p: (j, 0, 0))
    new = (shaped((count, rows, tile), BF), (1, rows, tile), lambda j, p: (j, 0, 0))
    return call(
        functools.partial(next_kernel, rows // BLOCK, per),
        count,
        ins,
        [new, product],
        12,
        (2 * tokens * rows * tile * count, 2 * rows * tile * count + 2 * tokens * rows),
        place,
    )


def finish_kernel(nbr, per, reps, place, keep_ref, send_ref, dec_ref, *refs):
    here = pl.program_id(0) % CORES == 0

    @pl.when(here)
    def _():
        refs[-1][...] = changed(keep_ref[0], dec_ref, refs[:reps], nbr, per)

    @pl.when(jnp.logical_not(here))
    def _():
        refs[-1][...] = changed(send_ref[0], dec_ref, refs[:reps], nbr, per)


def finish(place, keep, send, basis, coefs, per, start, total, previous):
    count, rows, tile = keep.shape
    each = lambda j, p: (j // CORES, 0, 0)
    return call(
        functools.partial(finish_kernel, rows // BLOCK, per, len(coefs)),
        count * CORES,
        [
            (keep, (1, rows, tile), each),
            (send, (1, rows, tile), each),
            (basis, (1,) + basis.shape[1:], lambda j, p: (CORES * start + j, 0, 0)),
        ]
        + [(coef, (1,) + coef.shape[1:], lambda j, p: (CORES * start + j, 0, 0)) for coef in coefs],
        [(shaped((rows, total), BF), (rows, tile), lambda j, p: (0, (CORES * start + j) ^ p[0]))],
        12,
        (2 * rows * 256 * tile * count * CORES, 4 * rows * tile * count * CORES),
        place,
        previous,
    )[0]


def by_distance(value, axes, index):
    for place, axis in enumerate(reversed(axes)):
        value = jnp.where((index >> place & 1) == 1, jnp.flip(value, axis), value)
    return value


def pick_tables(indices, step, reps, parts, replica, tp):
    nbr, nbc = indices.shape[2], indices.shape[3]
    per = nbc // parts * 2
    rep_bits, tp_bits = reps.bit_length() - 1, parts.bit_length() - 1
    picks = indices[step].reshape((2,) * rep_bits + (nbr,) + (2,) * tp_bits + (per,))
    picks = by_distance(picks, range(rep_bits), replica)
    picks = by_distance(picks, range(rep_bits + 1, rep_bits + 1 + tp_bits), tp)
    picks = picks.reshape(reps, nbr, parts, per).transpose(2, 0, 1, 3)
    picks = picks.reshape(parts, reps, nbr * per)
    both = jnp.concatenate([picks, picks + BLOCK], axis=2)
    own = jnp.concatenate([both[:, 0], picks[:, 0]], axis=1)
    return both.reshape(parts, 1, -1), own.reshape(parts, 1, -1), per


def local(reps, parts, inputs, targets, weight, momentum, indices):
    return steps(reps, parts, inputs, targets, weight, momentum, indices)


def steps(reps, parts, inputs, targets, weight, momentum, indices):
    rows, cols = weight.shape
    nbr = rows // BLOCK
    tile = cols // parts
    chips = parts // CORES
    count = chips // 2
    replica = lax.axis_index("rep").astype(jnp.int32)
    tp = lax.axis_index("tp").astype(jnp.int32)
    place = tp[None]

    acts_t, tables, projected = [None] * STEPS, [None] * STEPS, [None] * STEPS

    def basis_work(step, picked):
        picks_all, picks_own, per = pick_tables(picked, step, reps, parts, replica, tp)
        tables[step] = prep(place, picks_all, picks_own)
        projected[step], acts_t[step] = project(
            place, tables[step][2], inputs, step, nbr, per
        )
        return per

    moment = momentum
    gathered = None
    weights = [[None, None], [None, None]]
    final_m = final_w = None
    for step in range(STEPS):
        last = step == STEPS - 1
        totals = [None] * chips
        for chunk in (1, 0):
            start = chunk * count
            found = [None, None]
            for core in (1, 0):
                if step == 0:
                    found[core] = first(place, weight, inputs, tile, start, core, count)
                else:
                    weights[chunk][core], found[core] = forward(
                        place,
                        weight,
                        inputs,
                        step,
                        tile,
                        per,
                        start,
                        core,
                        count,
                        tables[step - 1][0],
                        gathered,
                    )
                if core == 1:
                    other = swap(found[1], "tp", parts, 1)
            for at in range(count):
                total = found[0][at].astype(F32) + other[at].astype(F32)
                totals[start + at] = total if start + at == 0 else total.astype(BF)
            if step == 0 and chunk == 1:
                *totals[count:], late = lax.optimization_barrier((*totals[count:], indices))
                for at in range(STEPS):
                    per = basis_work(at, late)
                old = moment_rows(place, tables[0][2], momentum, tile, per)
        total = totals[0] - targets[step].astype(F32)
        for mask in range(1, chips):
            total = total + swap(totals[mask], "tp", parts, mask * CORES).astype(F32)
        errors = lax.optimization_barrier(total.astype(BF))
        pieces = [errors] + [swap(errors, "tp", parts, mask * CORES) for mask in range(1, chips)]
        pairs = []
        for piece in pieces:
            pairs += [piece, swap(piece, "tp", parts, 1)]
        exact, sent = coefficients(place, projected[step], pairs, old)
        gathered = [sent] + [swap(sent, "rep", reps, mask) for mask in range(1, reps)]
        update = functools.partial(momentum_step, place, acts_t[step])
        if not last:
            moment, old = update(
                jnp.stack(pairs),
                moment,
                tables[step][1],
                exact,
                per,
                0,
                tables[step + 1][2],
                cols,
                None,
            )
        else:
            early, _ = coefficients(place, projected[step], pairs[:CORES], old)
            (final_m,) = update(
                jnp.stack(pairs[:CORES]),
                moment,
                tables[step][1],
                early,
                per,
                0,
                None,
                cols,
                None,
            )
            (final_m,) = update(
                jnp.stack(pairs[CORES:]),
                moment,
                tables[step][1],
                exact,
                per,
                CORES,
                None,
                cols,
                final_m,
            )
    for chunk in (0, 1):
        final_w = finish(
            place,
            weights[chunk][0],
            weights[chunk][1],
            tables[STEPS - 1][0],
            gathered,
            per,
            chunk * count,
            cols,
            final_w,
        )
    return (final_w, final_m)


def solution(mesh):
    reps, parts = mesh.shape["rep"], mesh.shape["tp"]
    in_specs = (
        P(None, "rep", "tp"),
        P(None, "rep", "tp"),
        P("tp", None),
        P("rep", "tp", None),
        P(None, None, "tp", None, None),
    )
    out_specs = (P("tp", None), P("rep", "tp", None))
    return jax.shard_map(
        functools.partial(local, reps, parts),
        mesh=mesh,
        in_specs=in_specs,
        out_specs=out_specs,
        check_vma=False,
    )
```

```python
import functools

import jax
import jax.numpy as jnp
import numpy as np
from jax import lax
from jax.experimental import pallas as pl
from jax.experimental.pallas import tpu as pltpu
from jax.sharding import PartitionSpec as P


BLOCK = 128
STEPS = 2
CORES = 2
BF = jnp.bfloat16
F32 = jnp.float32


def dct_table(size):
    rows = np.arange(size, dtype=np.float64)[:, None]
    cols = np.arange(size, dtype=np.float64)[None, :]
    scale = np.where(rows == 0, np.sqrt(1.0 / size), np.sqrt(2.0 / size))
    return (scale * np.cos(np.pi * (2.0 * cols + 1.0) * rows / (2.0 * size))).astype(np.float32)


def swap(value, axis, size, mask):
    return lax.ppermute(value, axis, [(at, at ^ mask) for at in range(size)])


def mask_at(position, chips):
    half = chips // 2
    return position % half * 2 + position // half


def dot(left, right):
    return lax.dot_general(left, right, (((1,), (0,)), ((), ())), preferred_element_type=F32)


def room(mib):
    return pltpu.CompilerParams(vmem_limit_bytes=mib << 20)


def cost(flops, moved):
    return pl.CostEstimate(flops=int(flops), bytes_accessed=int(moved), transcendentals=0)


def shaped(shape, dtype):
    return jax.ShapeDtypeStruct(shape, dtype)


def call(kernel, grid, ins, outs, mib, work, place, aliased=None):
    alias = {}
    arrays = [array for array, _, _ in ins]
    specs = [pl.BlockSpec(block, index) for _, block, index in ins]
    if aliased is not None:
        arrays.append(aliased)
        specs.append(pl.BlockSpec(memory_space=pl.ANY))
        alias = {len(arrays): 0}
    return pl.pallas_call(
        kernel,
        grid_spec=pltpu.PrefetchScalarGridSpec(
            num_scalar_prefetch=1,
            grid=(grid,),
            in_specs=specs,
            out_specs=[pl.BlockSpec(block, index) for _, block, index in outs],
        ),
        out_shape=[shape for shape, _, _ in outs],
        input_output_aliases=alias,
        compiler_params=room(mib),
        cost_estimate=cost(*work),
    )(place, *arrays)


def row_mask(rows, lanes, per, count, wanted, axis):
    return lax.broadcasted_iota(jnp.int32, (rows, lanes), axis) // per % count == wanted


def spread_rows(kept, nbr, per):
    kept = kept.astype(F32)
    return jnp.concatenate(
        [jnp.where(row_mask(*kept.shape, per, nbr, a, 0), kept, 0.0) for a in range(nbr)], axis=1
    ).astype(BF)


def spread_cols(basis, nbr, per):
    basis = basis.astype(F32)
    return jnp.concatenate(
        [jnp.where(row_mask(*basis.shape, per, nbr, a, 1), basis, 0.0) for a in range(nbr)], axis=0
    ).astype(BF)


def widen(coef, blocks):
    return jnp.concatenate(
        [jnp.where(row_mask(*coef.shape, 2, blocks, q, 0), coef, 0.0) for q in range(blocks)],
        axis=1,
    )


def narrow(wide, blocks):
    rows = wide.shape[0]
    return functools.reduce(
        jnp.add,
        [
            jnp.where(
                row_mask(rows, BLOCK, 2, blocks, q, 0), wide[:, q * BLOCK : (q + 1) * BLOCK], 0.0
            )
            for q in range(blocks)
        ],
    )


def fold(pair):
    half = pair.shape[0] // 2
    return pair[:half] + pair[half:]


def prep_kernel(place, all_ref, own_ref, cols_ref, rows_ref, dec_ref, own_dec_ref, kept_ref):
    wide = cols_ref.shape[1]

    def one_hot(picks):
        at = lax.broadcasted_iota(jnp.int32, (wide, picks.shape[-1]), 0)
        return (at == picks).astype(F32).astype(BF)

    dec_ref[0] = dot(cols_ref[...], one_hot(all_ref[0])).astype(BF)
    own = one_hot(own_ref[0])
    own_dec_ref[0] = dot(cols_ref[...], own).astype(BF)
    part = own.shape[1] // 3 * 2
    kept_ref[0] = lax.dot_general(
        own[:, :part], rows_ref[...], (((0,), (0,)), ((), ())), preferred_element_type=F32
    ).astype(BF)


def prep(place, picks_all, picks_own):
    tiles, _, width = picks_all.shape
    own = picks_own.shape[2]
    part = own // 3 * 2
    table = dct_table(BLOCK)
    high = np.asarray(table.astype(BF))
    low = np.asarray((table - high.astype(np.float32)).astype(BF))
    rows = jnp.asarray(np.concatenate([high, low], axis=0))
    cols = jnp.asarray(np.ascontiguousarray(np.concatenate([high, low], axis=0).T))
    each = lambda q, p: (q, 0, 0)
    once = lambda q, p: (0, 0)
    return call(
        prep_kernel,
        tiles,
        [
            (picks_all, (1, 1, width), each),
            (picks_own, (1, 1, own), each),
            (cols, cols.shape, once),
            (rows, rows.shape, once),
        ],
        [
            (shaped((tiles, BLOCK, width), BF), (1, BLOCK, width), each),
            (shaped((tiles, BLOCK, own), BF), (1, BLOCK, own), each),
            (shaped((tiles, part, BLOCK), BF), (1, part, BLOCK), each),
        ],
        4,
        (2 * tiles * 256 * 128 * (width + 2 * own), 2 << 20),
        place,
    )


def project_kernel(nbr, per, place, kept_ref, x_ref, out_ref, xt_ref):
    tiles = kept_ref.shape[0]
    xt_ref[...] = x_ref[0].T
    left = jnp.concatenate([spread_rows(kept_ref[q], nbr, per) for q in range(tiles)], axis=0)
    both = dot(left, xt_ref[...])
    pair = kept_ref.shape[1]
    for q in range(tiles):
        value = fold(both[q * pair : (q + 1) * pair])
        high = value.astype(BF)
        out_ref[q] = jnp.concatenate(
            [high.astype(F32), value - high.astype(F32)], axis=0
        ).astype(BF)


def project(place, kept, acts, step, nbr, per):
    tiles, pair, _ = kept.shape
    _, tokens, rows = acts.shape
    return call(
        functools.partial(project_kernel, nbr, per),
        1,
        [
            (kept, kept.shape, lambda j, p: (0, 0, 0)),
            (acts, (1, tokens, rows), lambda j, p: (step, 0, 0)),
        ],
        [
            (shaped((tiles, pair, tokens), BF), (tiles, pair, tokens), lambda j, p: (0, 0, 0)),
            (shaped((rows, tokens), BF), (rows, tokens), lambda j, p: (0, 0)),
        ],
        14,
        (2 * tiles * pair * rows * tokens, 4 * rows * tokens),
        place,
    )


def keep_rows(kept, moment, nbr, per, blocks):
    return narrow(fold(dot(spread_rows(kept, nbr, per), moment.astype(BF))), blocks)


def natural(position, tiles, place):
    return (mask_at(position // CORES, tiles // CORES) * CORES + position % CORES) ^ place[0]


def moment_rows_kernel(nbr, per, place, kept_ref, m_ref, out_ref):
    out_ref[0] = keep_rows(kept_ref[0], m_ref[0], nbr, per, m_ref.shape[2] // BLOCK)


def moment_rows(place, kept, momentum, tile, per):
    tiles, pair, _ = kept.shape
    rows = momentum.shape[1]
    return call(
        functools.partial(moment_rows_kernel, rows // BLOCK, per),
        tiles,
        [
            (kept, (1, pair, BLOCK), lambda j, p: (j, 0, 0)),
            (momentum, (1, rows, tile), lambda j, p: (0, 0, natural(j, tiles, p))),
        ],
        [(shaped((tiles, pair // 2, BLOCK), F32), (1, pair // 2, BLOCK), lambda j, p: (j, 0, 0))],
        8,
        (2 * tiles * pair * rows * tile, 4 * rows * tile * tiles),
        place,
    )[0]


def error_kernel(place, total_ref, goal_ref, *refs):
    *found, out_ref = refs
    total = total_ref[...] - goal_ref[0].astype(F32)
    for ref in found:
        total = total + ref[...].astype(F32)
    out_ref[...] = total.astype(BF)


def error_of(place, total, found, targets, step):
    shape = total.shape
    whole = lambda j, p: (0, 0)
    return call(
        error_kernel,
        1,
        [(total, shape, whole), (targets, (1,) + shape, lambda j, p: (step, 0, 0))]
        + [(piece, shape, whole) for piece in found],
        [(shaped(shape, BF), shape, whole)],
        6,
        (4 * total.size, 12 * total.size),
        place,
    )[0]


def coef_kernel(scale, place, proj_ref, old_ref, *refs):
    *e_refs, exact_ref, sent_ref = refs
    blocks = e_refs[0].shape[1] // BLOCK
    for q, e_ref in enumerate(e_refs):
        value = 0.9 * old_ref[q] + scale * narrow(fold(dot(proj_ref[q], e_ref[...])), blocks)
        exact_ref[q] = value
        sent_ref[q] = value.astype(BF)


def coefficients(place, proj, errors, old, position):
    tiles = len(errors)
    tokens, tile = errors[0].shape
    pair = proj.shape[1]
    shape = (tiles, pair // 2, BLOCK)
    at = lambda j, p: (position, 0, 0)
    whole = lambda j, p: (0, 0, 0)
    return call(
        functools.partial(coef_kernel, 1.0 / tokens),
        1,
        [(proj, (tiles, pair, tokens), at), (old, shape, at)]
        + [(piece, piece.shape, lambda j, p: (0, 0)) for piece in errors],
        [(shaped(shape, F32), shape, whole), (shaped(shape, BF), shape, whole)],
        8,
        (2 * tiles * pair * tokens * tile, 2 * tiles * tokens * tile),
        place,
    )


def momentum_kernel(scale, nbr, per, follow, place, xt_ref, e_ref, m_ref, dec_ref, coef_ref, *refs):
    refs = list(refs)
    kept_ref = refs.pop(0) if follow else None
    if len(refs) == 2 and not follow:
        refs.pop(0)
    coef = widen(coef_ref[0], m_ref.shape[2] // BLOCK)
    high = coef.astype(BF).astype(F32)
    back = jnp.concatenate([high, high, coef - high], axis=0).astype(BF)
    new = 0.9 * m_ref[0] + (
        dot(xt_ref[...], e_ref[0]) * scale - dot(spread_cols(dec_ref[0], nbr, per), back)
    )
    refs[0][0] = new
    if follow:
        refs[1][0] = keep_rows(kept_ref[0], new, nbr, per, new.shape[1] // BLOCK)


def momentum_step(
    place, acts_t, errors, moment, own_dec, coef, per, start, kept_next, total, previous
):
    rows, tokens = acts_t.shape
    tiles, _, tile = errors.shape
    nbr = rows // BLOCK
    follow = kept_next is not None
    each = lambda j, p: (start + j, 0, 0)
    here = lambda j, p: (j, 0, 0)
    columns = lambda j, p: (0, 0, natural(start + j, total // tile, p))
    ins = [
        (acts_t, acts_t.shape, lambda j, p: (0, 0)),
        (errors, (1, tokens, tile), here),
        (moment, (1, rows, tile), columns if moment.shape[0] == 1 else each),
        (own_dec, (1,) + own_dec.shape[1:], each),
        (coef, (1,) + coef.shape[1:], here),
    ]
    outs = []
    if follow:
        ins.append((kept_next, (1,) + kept_next.shape[1:], each))
        outs.append((shaped((tiles, rows, tile), F32), (1, rows, tile), here))
        outs.append((shaped(coef.shape, F32), (1,) + coef.shape[1:], here))
    else:
        outs.append((shaped((1, rows, total), F32), (1, rows, tile), columns))
    return call(
        functools.partial(momentum_kernel, 1.0 / tokens, nbr, per, follow),
        tiles,
        ins,
        outs,
        14,
        (2 * rows * tokens * tile * tiles, 8 * rows * tile * tiles),
        place,
        previous,
    )


def changed(weight, dec_ref, coef_refs, nbr, per):
    blocks = weight.shape[1] // BLOCK
    parts = []
    for coef_ref in coef_refs:
        parts += [widen(coef_ref[0].astype(F32), blocks)] * 2
    change = dot(spread_cols(dec_ref[0], nbr, per), jnp.concatenate(parts, axis=0).astype(BF))
    return (weight.astype(F32) - 0.1 * change).astype(BF)


def first_kernel(chips, start, core, place, w_ref, x_ref, out_ref, w_buf, x_buf, sum_ref, sems):
    count, rows, tile = w_buf.shape
    step = x_buf.shape[2]
    copies = []
    for k in range(rows // step):
        span = slice(k * step, (k + 1) * step)
        copies.append([])
        for at in range(count):
            column = natural(CORES * (start + at) + core, CORES * chips, place) * tile
            source = w_ref.at[span, pl.ds(pl.multiple_of(column, tile), tile)]
            target = w_buf.at[at, span, :]
            copies[k].append(pltpu.make_async_copy(source, target, sems.at[k, at]))
        source = x_ref.at[0, :, span]
        copies[k].append(pltpu.make_async_copy(source, x_buf.at[k], sems.at[k, count]))
    for group in copies:
        for copy in group:
            copy.start()
    for k, group in enumerate(copies):
        span = slice(k * step, (k + 1) * step)
        for copy in group:
            copy.wait()
        for at in range(count):
            part = dot(x_buf[k], w_buf[at, span, :])
            if k > 0:
                part = part + sum_ref[at]
            if k < len(copies) - 1:
                sum_ref[at] = part
            else:
                out_ref[at] = part.astype(BF)


def first(place, weight, acts, tile, start, core, count):
    rows = weight.shape[0]
    tokens = acts.shape[1]
    step = 256
    hbm = pl.BlockSpec(memory_space=pltpu.HBM)
    return pl.pallas_call(
        functools.partial(first_kernel, weight.shape[1] // tile // CORES, start, core),
        grid_spec=pltpu.PrefetchScalarGridSpec(
            num_scalar_prefetch=1,
            grid=(1,),
            in_specs=[hbm, hbm],
            out_specs=pl.BlockSpec((count, tokens, tile), lambda j, p: (0, 0, 0)),
            scratch_shapes=[
                pltpu.VMEM((count, rows, tile), BF),
                pltpu.VMEM((rows // step, tokens, step), BF),
                pltpu.VMEM((count, tokens, tile), F32),
                pltpu.SemaphoreType.DMA((rows // step, count + 1)),
            ],
        ),
        out_shape=shaped((count, tokens, tile), BF),
        compiler_params=room(52),
        cost_estimate=cost(2 * tokens * rows * tile * count, 2 * rows * (tile * count + tokens)),
        name="first",
    )(place, weight, acts)


def next_kernel(nbr, per, place, w_ref, x_ref, dec_ref, *refs):
    *coef_refs, new_ref, out_ref = refs
    new = changed(w_ref[...], dec_ref, coef_refs, nbr, per)
    new_ref[0] = new
    out_ref[0] = dot(x_ref[0], new).astype(BF)


def forward(place, weight, acts, step, tile, per, start, core, count, basis, coefs):
    rows = weight.shape[0]
    tokens = acts.shape[1]
    at = lambda j: CORES * (start + j) + core
    ins = [
        (weight, (rows, tile), lambda j, p: (0, natural(at(j), weight.shape[1] // tile, p))),
        (acts, (1, tokens, rows), lambda j, p: (step, 0, 0)),
        (basis, (1,) + basis.shape[1:], lambda j, p: (at(j), 0, 0)),
    ]
    for coef in coefs:
        ins.append((coef, (1,) + coef.shape[1:], lambda j, p: (CORES * j + core, 0, 0)))
    product = (shaped((count, tokens, tile), BF), (1, tokens, tile), lambda j, p: (j, 0, 0))
    new = (shaped((count, rows, tile), BF), (1, rows, tile), lambda j, p: (j, 0, 0))
    return call(
        functools.partial(next_kernel, rows // BLOCK, per),
        count,
        ins,
        [new, product],
        12,
        (2 * tokens * rows * tile * count, 2 * rows * tile * count + 2 * tokens * rows),
        place,
    )


def finish_kernel(nbr, per, reps, place, keep_ref, send_ref, dec_ref, *refs):
    here = pl.program_id(0) % CORES == 0

    @pl.when(here)
    def _():
        refs[-1][...] = changed(keep_ref[0], dec_ref, refs[:reps], nbr, per)

    @pl.when(jnp.logical_not(here))
    def _():
        refs[-1][...] = changed(send_ref[0], dec_ref, refs[:reps], nbr, per)


def finish(place, keep, send, basis, coefs, per, start, total, previous):
    count, rows, tile = keep.shape
    each = lambda j, p: (j // CORES, 0, 0)
    return call(
        functools.partial(finish_kernel, rows // BLOCK, per, len(coefs)),
        count * CORES,
        [
            (keep, (1, rows, tile), each),
            (send, (1, rows, tile), each),
            (basis, (1,) + basis.shape[1:], lambda j, p: (CORES * start + j, 0, 0)),
        ]
        + [(coef, (1,) + coef.shape[1:], lambda j, p: (j, 0, 0)) for coef in coefs],
        [
            (
                shaped((rows, total), BF),
                (rows, tile),
                lambda j, p: (0, natural(CORES * start + j, total // tile, p)),
            )
        ],
        12,
        (2 * rows * 256 * tile * count * CORES, 4 * rows * tile * count * CORES),
        place,
        previous,
    )[0]


def by_distance(value, axes, index):
    for place, axis in enumerate(reversed(axes)):
        value = jnp.where((index >> place & 1) == 1, jnp.flip(value, axis), value)
    return value


def pick_tables(indices, step, reps, parts, replica, tp):
    nbr, nbc = indices.shape[2], indices.shape[3]
    per = nbc // parts * 2
    rep_bits, tp_bits = reps.bit_length() - 1, parts.bit_length() - 1
    picks = indices[step].reshape((2,) * rep_bits + (nbr,) + (2,) * tp_bits + (per,))
    picks = by_distance(picks, range(rep_bits), replica)
    picks = by_distance(picks, range(rep_bits + 1, rep_bits + 1 + tp_bits), tp)
    picks = picks.reshape(reps, nbr, parts // CORES // 2, 2, CORES, per)
    picks = picks.transpose(3, 2, 4, 0, 1, 5)
    picks = picks.reshape(parts, reps, nbr * per)
    both = jnp.concatenate([picks, picks + BLOCK], axis=2)
    own = jnp.concatenate([both[:, 0], picks[:, 0]], axis=1)
    return both.reshape(parts, 1, -1), own.reshape(parts, 1, -1), per


def local(reps, parts, inputs, targets, weight, momentum, indices):
    return steps(reps, parts, inputs, targets, weight, momentum, indices)


def steps(reps, parts, inputs, targets, weight, momentum, indices):
    rows, cols = weight.shape
    nbr = rows // BLOCK
    tile = cols // parts
    chips = parts // CORES
    count = chips // 2
    replica = lax.axis_index("rep").astype(jnp.int32)
    tp = lax.axis_index("tp").astype(jnp.int32)
    place = tp[None]

    acts_t, tables, projected = [None] * STEPS, [None] * STEPS, [None] * STEPS
    chunks = (0, 1)
    mask_of = [mask_at(position, chips) for position in range(chips)]

    def basis_work(picked):
        for step in range(STEPS):
            picks_all, picks_own, per = pick_tables(picked, step, reps, parts, replica, tp)
            tables[step] = prep(place, picks_all, picks_own)
            projected[step], acts_t[step] = project(place, tables[step][2], inputs, step, nbr, per)
        return moment_rows(place, tables[0][2], momentum, tile, per), per

    moment = momentum
    gathered = [None, None]
    weights = [[None, None], [None, None]]
    final_m = final_w = None
    for step in range(STEPS):
        last = step == STEPS - 1
        found_all = []
        for chunk in chunks:
            start = chunk * count
            found = [None, None]
            for core in (1, 0):
                if step == 0:
                    found[core] = first(place, weight, inputs, tile, start, core, count)
                else:
                    weights[chunk][core], found[core] = forward(
                        place,
                        weight,
                        inputs,
                        step,
                        tile,
                        per,
                        start,
                        core,
                        count,
                        tables[step - 1][0],
                        gathered[chunk],
                    )
                if core == 1:
                    other = swap(found[1], "tp", parts, 1)
            sums = [found[0][at].astype(F32) + other[at].astype(F32) for at in range(count)]
            if chunk == 0:
                total, sums = sums[0], [None] + [value.astype(BF) for value in sums[1:]]
                if step == 0:
                    *sums[1:], late = lax.optimization_barrier((*sums[1:], indices))
                    old, per = basis_work(late)
            for at, value in enumerate(sums):
                mask = mask_of[start + at]
                if mask:
                    found_all.append(swap(value.astype(BF), "tp", parts, mask * CORES))
        errors = error_of(place, total, found_all, targets, step)
        pairs, exact, sent = [], [], []
        for position, mask in enumerate(mask_of):
            piece = errors
            if mask:
                piece = swap(errors, "tp", parts, mask * CORES)
            pair = [piece, swap(piece, "tp", parts, 1)]
            value, small = coefficients(place, projected[step], pair, old, position)
            pairs += pair
            exact.append(value)
            sent.append(small)
        for chunk in chunks:
            both = jnp.concatenate(sent[chunk * count : (chunk + 1) * count])
            gathered[chunk] = [both] + [swap(both, "rep", reps, mask) for mask in range(1, reps)]
        update = functools.partial(momentum_step, place, acts_t[step])
        if not last:
            moment, old = update(
                jnp.stack(pairs),
                moment,
                tables[step][1],
                jnp.concatenate(exact),
                per,
                0,
                tables[step + 1][2],
                cols,
                None,
            )
        else:
            for chunk in chunks:
                (final_m,) = update(
                    jnp.stack(pairs[chunk * count * CORES : (chunk + 1) * count * CORES]),
                    moment,
                    tables[step][1],
                    jnp.concatenate(exact[chunk * count : (chunk + 1) * count]),
                    per,
                    chunk * count * CORES,
                    None,
                    cols,
                    final_m,
                )
    for chunk in chunks:
        final_w = finish(
            place,
            weights[chunk][0],
            weights[chunk][1],
            tables[STEPS - 1][0],
            gathered[chunk],
            per,
            chunk * count,
            cols,
            final_w,
        )
    return (final_w, final_m)


def solution(mesh):
    reps, parts = mesh.shape["rep"], mesh.shape["tp"]
    in_specs = (
        P(None, "rep", "tp"),
        P(None, "rep", "tp"),
        P("tp", None),
        P("rep", "tp", None),
        P(None, None, "tp", None, None),
    )
    out_specs = (P("tp", None), P("rep", "tp", None))
    return jax.shard_map(
        functools.partial(local, reps, parts),
        mesh=mesh,
        in_specs=in_specs,
        out_specs=out_specs,
        check_vma=False,
    )
```

```python
import functools

import jax
import jax.numpy as jnp
import numpy as np
from jax import lax
from jax.experimental import pallas as pl
from jax.experimental.pallas import tpu as pltpu
from jax.sharding import PartitionSpec as P


BLOCK = 128
STEPS = 2
CORES = 2
BF = jnp.bfloat16
F32 = jnp.float32


def dct_table(size):
    rows = np.arange(size, dtype=np.float64)[:, None]
    cols = np.arange(size, dtype=np.float64)[None, :]
    scale = np.where(rows == 0, np.sqrt(1.0 / size), np.sqrt(2.0 / size))
    return (scale * np.cos(np.pi * (2.0 * cols + 1.0) * rows / (2.0 * size))).astype(np.float32)


def swap(value, axis, size, mask):
    return lax.ppermute(value, axis, [(at, at ^ mask) for at in range(size)])


def mask_at(position, chips):
    half = chips // 2
    return position % half * 2 + position // half


def dot(left, right):
    return lax.dot_general(left, right, (((1,), (0,)), ((), ())), preferred_element_type=F32)


def room(mib):
    return pltpu.CompilerParams(vmem_limit_bytes=mib << 20)


def cost(flops, moved):
    return pl.CostEstimate(flops=int(flops), bytes_accessed=int(moved), transcendentals=0)


def shaped(shape, dtype):
    return jax.ShapeDtypeStruct(shape, dtype)


def call(kernel, grid, ins, outs, mib, work, place, aliased=None):
    alias = {}
    arrays = [array for array, _, _ in ins]
    specs = [pl.BlockSpec(block, index) for _, block, index in ins]
    if aliased is not None:
        arrays.append(aliased)
        specs.append(pl.BlockSpec(memory_space=pl.ANY))
        alias = {len(arrays): 0}
    return pl.pallas_call(
        kernel,
        grid_spec=pltpu.PrefetchScalarGridSpec(
            num_scalar_prefetch=1,
            grid=(grid,),
            in_specs=specs,
            out_specs=[pl.BlockSpec(block, index) for _, block, index in outs],
        ),
        out_shape=[shape for shape, _, _ in outs],
        input_output_aliases=alias,
        compiler_params=room(mib),
        cost_estimate=cost(*work),
    )(place, *arrays)


def row_mask(rows, lanes, per, count, wanted, axis):
    return lax.broadcasted_iota(jnp.int32, (rows, lanes), axis) // per % count == wanted


def spread_rows(kept, nbr, per):
    kept = kept.astype(F32)
    return jnp.concatenate(
        [jnp.where(row_mask(*kept.shape, per, nbr, a, 0), kept, 0.0) for a in range(nbr)], axis=1
    ).astype(BF)


def spread_cols(basis, nbr, per):
    basis = basis.astype(F32)
    return jnp.concatenate(
        [jnp.where(row_mask(*basis.shape, per, nbr, a, 1), basis, 0.0) for a in range(nbr)], axis=0
    ).astype(BF)


def widen(coef, blocks):
    return jnp.concatenate(
        [jnp.where(row_mask(*coef.shape, 2, blocks, q, 0), coef, 0.0) for q in range(blocks)],
        axis=1,
    )


def narrow(wide, blocks):
    rows = wide.shape[0]
    return functools.reduce(
        jnp.add,
        [
            jnp.where(
                row_mask(rows, BLOCK, 2, blocks, q, 0), wide[:, q * BLOCK : (q + 1) * BLOCK], 0.0
            )
            for q in range(blocks)
        ],
    )


def fold(pair):
    half = pair.shape[0] // 2
    return pair[:half] + pair[half:]


def prep_kernel(place, all_ref, own_ref, cols_ref, rows_ref, dec_ref, own_dec_ref, kept_ref):
    wide = cols_ref.shape[1]

    def one_hot(picks):
        at = lax.broadcasted_iota(jnp.int32, (wide, picks.shape[-1]), 0)
        return (at == picks).astype(F32).astype(BF)

    dec_ref[0] = dot(cols_ref[...], one_hot(all_ref[0])).astype(BF)
    own = one_hot(own_ref[0])
    own_dec_ref[0] = dot(cols_ref[...], own).astype(BF)
    part = own.shape[1] // 3 * 2
    kept_ref[0] = lax.dot_general(
        own[:, :part], rows_ref[...], (((0,), (0,)), ((), ())), preferred_element_type=F32
    ).astype(BF)


def prep(place, picks_all, picks_own):
    tiles, _, width = picks_all.shape
    own = picks_own.shape[2]
    part = own // 3 * 2
    table = dct_table(BLOCK)
    high = np.asarray(table.astype(BF))
    low = np.asarray((table - high.astype(np.float32)).astype(BF))
    rows = jnp.asarray(np.concatenate([high, low], axis=0))
    cols = jnp.asarray(np.ascontiguousarray(np.concatenate([high, low], axis=0).T))
    each = lambda q, p: (q, 0, 0)
    once = lambda q, p: (0, 0)
    return call(
        prep_kernel,
        tiles,
        [
            (picks_all, (1, 1, width), each),
            (picks_own, (1, 1, own), each),
            (cols, cols.shape, once),
            (rows, rows.shape, once),
        ],
        [
            (shaped((tiles, BLOCK, width), BF), (1, BLOCK, width), each),
            (shaped((tiles, BLOCK, own), BF), (1, BLOCK, own), each),
            (shaped((tiles, part, BLOCK), BF), (1, part, BLOCK), each),
        ],
        4,
        (2 * tiles * 256 * 128 * (width + 2 * own), 2 << 20),
        place,
    )


def project_kernel(nbr, per, place, kept_ref, x_ref, out_ref, xt_ref):
    tiles = kept_ref.shape[0]
    xt_ref[...] = x_ref[0].T
    left = jnp.concatenate([spread_rows(kept_ref[q], nbr, per) for q in range(tiles)], axis=0)
    both = dot(left, xt_ref[...])
    pair = kept_ref.shape[1]
    for q in range(tiles):
        value = fold(both[q * pair : (q + 1) * pair])
        high = value.astype(BF)
        out_ref[q] = jnp.concatenate(
            [high.astype(F32), value - high.astype(F32)], axis=0
        ).astype(BF)


def project(place, kept, acts, step, nbr, per):
    tiles, pair, _ = kept.shape
    _, tokens, rows = acts.shape
    return call(
        functools.partial(project_kernel, nbr, per),
        1,
        [
            (kept, kept.shape, lambda j, p: (0, 0, 0)),
            (acts, (1, tokens, rows), lambda j, p: (step, 0, 0)),
        ],
        [
            (shaped((tiles, pair, tokens), BF), (tiles, pair, tokens), lambda j, p: (0, 0, 0)),
            (shaped((rows, tokens), BF), (rows, tokens), lambda j, p: (0, 0)),
        ],
        14,
        (2 * tiles * pair * rows * tokens, 4 * rows * tokens),
        place,
    )


def keep_rows(kept, moment, nbr, per, blocks):
    return narrow(fold(dot(spread_rows(kept, nbr, per), moment.astype(BF))), blocks)


def natural(position, tiles, place):
    return (mask_at(position // CORES, tiles // CORES) * CORES + position % CORES) ^ place[0]


def moment_rows_kernel(nbr, per, place, kept_ref, m_ref, out_ref):
    out_ref[0] = keep_rows(kept_ref[0], m_ref[0], nbr, per, m_ref.shape[2] // BLOCK)


def moment_rows(place, kept, momentum, tile, per):
    tiles, pair, _ = kept.shape
    rows = momentum.shape[1]
    return call(
        functools.partial(moment_rows_kernel, rows // BLOCK, per),
        tiles,
        [
            (kept, (1, pair, BLOCK), lambda j, p: (j, 0, 0)),
            (momentum, (1, rows, tile), lambda j, p: (0, 0, natural(j, tiles, p))),
        ],
        [(shaped((tiles, pair // 2, BLOCK), F32), (1, pair // 2, BLOCK), lambda j, p: (j, 0, 0))],
        8,
        (2 * tiles * pair * rows * tile, 4 * rows * tile * tiles),
        place,
    )[0]


def error_kernel(place, total_ref, goal_ref, *refs):
    *found, out_ref = refs
    total = total_ref[...] - goal_ref[0].astype(F32)
    for ref in found:
        total = total + ref[...].astype(F32)
    out_ref[...] = total.astype(BF)


def error_of(place, total, found, targets, step):
    shape = total.shape
    whole = lambda j, p: (0, 0)
    return call(
        error_kernel,
        1,
        [(total, shape, whole), (targets, (1,) + shape, lambda j, p: (step, 0, 0))]
        + [(piece, shape, whole) for piece in found],
        [(shaped(shape, BF), shape, whole)],
        6,
        (4 * total.size, 12 * total.size),
        place,
    )[0]


def coef_kernel(scale, place, proj_ref, old_ref, *refs):
    *e_refs, exact_ref, sent_ref = refs
    blocks = e_refs[0].shape[1] // BLOCK
    for q, e_ref in enumerate(e_refs):
        value = 0.9 * old_ref[q] + scale * narrow(fold(dot(proj_ref[q], e_ref[...])), blocks)
        exact_ref[q] = value
        sent_ref[q] = value.astype(BF)


def coefficients(place, proj, errors, old, position):
    tiles = len(errors)
    tokens, tile = errors[0].shape
    pair = proj.shape[1]
    shape = (tiles, pair // 2, BLOCK)
    at = lambda j, p: (position, 0, 0)
    whole = lambda j, p: (0, 0, 0)
    return call(
        functools.partial(coef_kernel, 1.0 / tokens),
        1,
        [(proj, (tiles, pair, tokens), at), (old, shape, at)]
        + [(piece, piece.shape, lambda j, p: (0, 0)) for piece in errors],
        [(shaped(shape, F32), shape, whole), (shaped(shape, BF), shape, whole)],
        8,
        (2 * tiles * pair * tokens * tile, 2 * tiles * tokens * tile),
        place,
    )


def momentum_kernel(scale, nbr, per, follow, place, xt_ref, e_ref, m_ref, dec_ref, coef_ref, *refs):
    refs = list(refs)
    kept_ref = refs.pop(0) if follow else None
    if len(refs) == 2 and not follow:
        refs.pop(0)
    coef = widen(coef_ref[0], m_ref.shape[2] // BLOCK)
    high = coef.astype(BF).astype(F32)
    back = jnp.concatenate([high, high, coef - high], axis=0).astype(BF)
    new = 0.9 * m_ref[0] + (
        dot(xt_ref[...], e_ref[0]) * scale - dot(spread_cols(dec_ref[0], nbr, per), back)
    )
    refs[0][0] = new
    if follow:
        refs[1][0] = keep_rows(kept_ref[0], new, nbr, per, new.shape[1] // BLOCK)


def momentum_step(
    place, acts_t, errors, moment, own_dec, coef, per, start, kept_next, total, previous
):
    rows, tokens = acts_t.shape
    tiles, _, tile = errors.shape
    nbr = rows // BLOCK
    follow = kept_next is not None
    each = lambda j, p: (start + j, 0, 0)
    here = lambda j, p: (j, 0, 0)
    columns = lambda j, p: (0, 0, natural(start + j, total // tile, p))
    ins = [
        (acts_t, acts_t.shape, lambda j, p: (0, 0)),
        (errors, (1, tokens, tile), here),
        (moment, (1, rows, tile), columns if moment.shape[0] == 1 else each),
        (own_dec, (1,) + own_dec.shape[1:], each),
        (coef, (1,) + coef.shape[1:], here),
    ]
    outs = []
    if follow:
        ins.append((kept_next, (1,) + kept_next.shape[1:], each))
        outs.append((shaped((tiles, rows, tile), F32), (1, rows, tile), here))
        outs.append((shaped(coef.shape, F32), (1,) + coef.shape[1:], here))
    else:
        outs.append((shaped((1, rows, total), F32), (1, rows, tile), columns))
    return call(
        functools.partial(momentum_kernel, 1.0 / tokens, nbr, per, follow),
        tiles,
        ins,
        outs,
        14,
        (2 * rows * tokens * tile * tiles, 8 * rows * tile * tiles),
        place,
        previous,
    )


def changed(weight, dec_ref, coef_refs, nbr, per):
    blocks = weight.shape[1] // BLOCK
    parts = []
    for coef_ref in coef_refs:
        parts += [widen(coef_ref[0].astype(F32), blocks)] * 2
    change = dot(spread_cols(dec_ref[0], nbr, per), jnp.concatenate(parts, axis=0).astype(BF))
    return (weight.astype(F32) - 0.1 * change).astype(BF)


def first_kernel(chips, start, core, place, w_ref, x_ref, out_ref, w_buf, x_buf, sum_ref, sems):
    count, rows, tile = w_buf.shape
    step = x_buf.shape[2]
    copies = []
    for k in range(rows // step):
        span = slice(k * step, (k + 1) * step)
        copies.append([])
        for at in range(count):
            column = natural(CORES * (start + at) + core, CORES * chips, place) * tile
            source = w_ref.at[span, pl.ds(pl.multiple_of(column, tile), tile)]
            target = w_buf.at[at, span, :]
            copies[k].append(pltpu.make_async_copy(source, target, sems.at[k, at]))
        source = x_ref.at[0, :, span]
        copies[k].append(pltpu.make_async_copy(source, x_buf.at[k], sems.at[k, count]))
    for group in copies:
        for copy in group:
            copy.start()
    for k, group in enumerate(copies):
        span = slice(k * step, (k + 1) * step)
        for copy in group:
            copy.wait()
        for at in range(count):
            part = dot(x_buf[k], w_buf[at, span, :])
            if k > 0:
                part = part + sum_ref[at]
            if k < len(copies) - 1:
                sum_ref[at] = part
            else:
                out_ref[at] = part.astype(BF)


def first(place, weight, acts, tile, start, core, count):
    rows = weight.shape[0]
    tokens = acts.shape[1]
    step = 256
    hbm = pl.BlockSpec(memory_space=pltpu.HBM)
    return pl.pallas_call(
        functools.partial(first_kernel, weight.shape[1] // tile // CORES, start, core),
        grid_spec=pltpu.PrefetchScalarGridSpec(
            num_scalar_prefetch=1,
            grid=(1,),
            in_specs=[hbm, hbm],
            out_specs=pl.BlockSpec((count, tokens, tile), lambda j, p: (0, 0, 0)),
            scratch_shapes=[
                pltpu.VMEM((count, rows, tile), BF),
                pltpu.VMEM((rows // step, tokens, step), BF),
                pltpu.VMEM((count, tokens, tile), F32),
                pltpu.SemaphoreType.DMA((rows // step, count + 1)),
            ],
        ),
        out_shape=shaped((count, tokens, tile), BF),
        compiler_params=room(52),
        cost_estimate=cost(2 * tokens * rows * tile * count, 2 * rows * (tile * count + tokens)),
        name="first",
    )(place, weight, acts)


def next_kernel(nbr, per, place, w_ref, x_ref, dec_ref, *refs):
    *coef_refs, new_ref, out_ref = refs
    new = changed(w_ref[...], dec_ref, coef_refs, nbr, per)
    new_ref[0] = new
    out_ref[0] = dot(x_ref[0], new).astype(BF)


def forward(place, weight, acts, step, tile, per, start, core, count, basis, coefs, skip):
    rows = weight.shape[0]
    tokens = acts.shape[1]
    at = lambda j: CORES * (start + j) + core
    ins = [
        (weight, (rows, tile), lambda j, p: (0, natural(at(j), weight.shape[1] // tile, p))),
        (acts, (1, tokens, rows), lambda j, p: (step, 0, 0)),
        (basis, (1,) + basis.shape[1:], lambda j, p: (at(j), 0, 0)),
    ]
    for coef in coefs:
        ins.append((coef, (1,) + coef.shape[1:], lambda j, p: (CORES * (skip + j) + core, 0, 0)))
    product = (shaped((count, tokens, tile), BF), (1, tokens, tile), lambda j, p: (j, 0, 0))
    new = (shaped((count, rows, tile), BF), (1, rows, tile), lambda j, p: (j, 0, 0))
    return call(
        functools.partial(next_kernel, rows // BLOCK, per),
        count,
        ins,
        [new, product],
        12,
        (2 * tokens * rows * tile * count, 2 * rows * tile * count + 2 * tokens * rows),
        place,
    )


def finish_kernel(nbr, per, reps, place, keep_ref, send_ref, dec_ref, *refs):
    here = pl.program_id(0) % CORES == 0

    @pl.when(here)
    def _():
        refs[-1][...] = changed(keep_ref[0], dec_ref, refs[:reps], nbr, per)

    @pl.when(jnp.logical_not(here))
    def _():
        refs[-1][...] = changed(send_ref[0], dec_ref, refs[:reps], nbr, per)


def finish(place, keep, send, basis, coefs, per, start, total, previous, skip):
    count, rows, tile = keep.shape
    each = lambda j, p: (j // CORES, 0, 0)
    return call(
        functools.partial(finish_kernel, rows // BLOCK, per, len(coefs)),
        count * CORES,
        [
            (keep, (1, rows, tile), each),
            (send, (1, rows, tile), each),
            (basis, (1,) + basis.shape[1:], lambda j, p: (CORES * start + j, 0, 0)),
        ]
        + [(coef, (1,) + coef.shape[1:], lambda j, p: (CORES * skip + j, 0, 0)) for coef in coefs],
        [
            (
                shaped((rows, total), BF),
                (rows, tile),
                lambda j, p: (0, natural(CORES * start + j, total // tile, p)),
            )
        ],
        12,
        (2 * rows * 256 * tile * count * CORES, 4 * rows * tile * count * CORES),
        place,
        previous,
    )[0]


def by_distance(value, axes, index):
    for place, axis in enumerate(reversed(axes)):
        value = jnp.where((index >> place & 1) == 1, jnp.flip(value, axis), value)
    return value


def pick_tables(indices, step, reps, parts, replica, tp):
    nbr, nbc = indices.shape[2], indices.shape[3]
    per = nbc // parts * 2
    rep_bits, tp_bits = reps.bit_length() - 1, parts.bit_length() - 1
    picks = indices[step].reshape((2,) * rep_bits + (nbr,) + (2,) * tp_bits + (per,))
    picks = by_distance(picks, range(rep_bits), replica)
    picks = by_distance(picks, range(rep_bits + 1, rep_bits + 1 + tp_bits), tp)
    picks = picks.reshape(reps, nbr, parts // CORES // 2, 2, CORES, per)
    picks = picks.transpose(3, 2, 4, 0, 1, 5)
    picks = picks.reshape(parts, reps, nbr * per)
    both = jnp.concatenate([picks, picks + BLOCK], axis=2)
    own = jnp.concatenate([both[:, 0], picks[:, 0]], axis=1)
    return both.reshape(parts, 1, -1), own.reshape(parts, 1, -1), per


def local(reps, parts, inputs, targets, weight, momentum, indices):
    return steps(reps, parts, inputs, targets, weight, momentum, indices)


def steps(reps, parts, inputs, targets, weight, momentum, indices):
    rows, cols = weight.shape
    nbr = rows // BLOCK
    tile = cols // parts
    chips = parts // CORES
    count = chips // 2
    replica = lax.axis_index("rep").astype(jnp.int32)
    tp = lax.axis_index("tp").astype(jnp.int32)
    place = tp[None]

    acts_t, tables, projected = [None] * STEPS, [None] * STEPS, [None] * STEPS
    chunks = (0, 1)
    mask_of = [mask_at(position, chips) for position in range(chips)]
    groups = ((1, count - 1, 0, 1), (count, count, 1, 0), (0, 1, 0, 0))

    def basis_work(picked):
        for step in range(STEPS):
            picks_all, picks_own, per = pick_tables(picked, step, reps, parts, replica, tp)
            tables[step] = prep(place, picks_all, picks_own)
            projected[step], acts_t[step] = project(place, tables[step][2], inputs, step, nbr, per)
        return moment_rows(place, tables[0][2], momentum, tile, per), per

    moment = momentum
    gathered = [None, None]
    weights = [[None, None] for _ in groups]
    final_m = final_w = None
    for step in range(STEPS):
        last = step == STEPS - 1
        found_all = []
        for group, (start, size, chunk, skip) in enumerate(groups):
            found = [None, None]
            for core in (1, 0):
                if step == 0:
                    found[core] = first(place, weight, inputs, tile, start, core, size)
                else:
                    weights[group][core], found[core] = forward(
                        place,
                        weight,
                        inputs,
                        step,
                        tile,
                        per,
                        start,
                        core,
                        size,
                        tables[step - 1][0],
                        gathered[chunk],
                        skip,
                    )
                if core == 1:
                    other = swap(found[1], "tp", parts, 1)
            sums = [found[0][at].astype(F32) + other[at].astype(F32) for at in range(size)]
            if start == 0:
                total = sums[0]
                continue
            sums = [value.astype(BF) for value in sums]
            if step == 0 and group == 1:
                *sums, late = lax.optimization_barrier((*sums, indices))
                old, per = basis_work(late)
            for at, value in enumerate(sums):
                mask = mask_of[start + at]
                found_all.append(swap(value, "tp", parts, mask * CORES))
        errors = error_of(place, total, found_all, targets, step)
        pairs, exact, sent = [], [], []
        for position, mask in enumerate(mask_of):
            piece = errors
            if mask:
                piece = swap(errors, "tp", parts, mask * CORES)
            pair = [piece, swap(piece, "tp", parts, 1)]
            value, small = coefficients(place, projected[step], pair, old, position)
            pairs += pair
            exact.append(value)
            sent.append(small)
        for chunk in chunks:
            both = jnp.concatenate(sent[chunk * count : (chunk + 1) * count])
            gathered[chunk] = [both] + [swap(both, "rep", reps, mask) for mask in range(1, reps)]
        update = functools.partial(momentum_step, place, acts_t[step])
        if not last:
            moment, old = update(
                jnp.stack(pairs),
                moment,
                tables[step][1],
                jnp.concatenate(exact),
                per,
                0,
                tables[step + 1][2],
                cols,
                None,
            )
        else:
            for start, size in ((0, 1), (1, count - 1), (count, count)):
                (final_m,) = update(
                    jnp.stack(pairs[start * CORES : (start + size) * CORES]),
                    moment,
                    tables[step][1],
                    jnp.concatenate(exact[start : start + size]),
                    per,
                    start * CORES,
                    None,
                    cols,
                    final_m,
                )
    for group in (2, 0, 1):
        start, _, chunk, skip = groups[group]
        final_w = finish(
            place,
            weights[group][0],
            weights[group][1],
            tables[STEPS - 1][0],
            gathered[chunk],
            per,
            start,
            cols,
            final_w,
            skip,
        )
    return (final_w, final_m)


def solution(mesh):
    reps, parts = mesh.shape["rep"], mesh.shape["tp"]
    in_specs = (
        P(None, "rep", "tp"),
        P(None, "rep", "tp"),
        P("tp", None),
        P("rep", "tp", None),
        P(None, None, "tp", None, None),
    )
    out_specs = (P("tp", None), P("rep", "tp", None))
    return jax.shard_map(
        functools.partial(local, reps, parts),
        mesh=mesh,
        in_specs=in_specs,
        out_specs=out_specs,
        check_vma=False,
    )
```

```python
import functools

import jax
import jax.numpy as jnp
import numpy as np
from jax import lax
from jax.experimental import pallas as pl
from jax.experimental.pallas import tpu as pltpu
from jax.sharding import PartitionSpec as P


BLOCK = 128
STEPS = 2
CORES = 2
BF = jnp.bfloat16
F32 = jnp.float32


def dct_table(size):
    rows = np.arange(size, dtype=np.float64)[:, None]
    cols = np.arange(size, dtype=np.float64)[None, :]
    scale = np.where(rows == 0, np.sqrt(1.0 / size), np.sqrt(2.0 / size))
    return (scale * np.cos(np.pi * (2.0 * cols + 1.0) * rows / (2.0 * size))).astype(np.float32)


def swap(value, axis, size, mask):
    return lax.ppermute(value, axis, [(at, at ^ mask) for at in range(size)])


def mask_at(position, chips):
    half = chips // 2
    return position % half * 2 + position // half


def dot(left, right):
    return lax.dot_general(left, right, (((1,), (0,)), ((), ())), preferred_element_type=F32)


def room(mib):
    return pltpu.CompilerParams(vmem_limit_bytes=mib << 20)


def cost(flops, moved):
    return pl.CostEstimate(flops=int(flops), bytes_accessed=int(moved), transcendentals=0)


def shaped(shape, dtype):
    return jax.ShapeDtypeStruct(shape, dtype)


def call(kernel, grid, ins, outs, mib, work, place, aliased=None):
    alias = {}
    arrays = [array for array, _, _ in ins]
    specs = [pl.BlockSpec(block, index) for _, block, index in ins]
    if aliased is not None:
        arrays.append(aliased)
        specs.append(pl.BlockSpec(memory_space=pl.ANY))
        alias = {len(arrays): 0}
    return pl.pallas_call(
        kernel,
        grid_spec=pltpu.PrefetchScalarGridSpec(
            num_scalar_prefetch=1,
            grid=(grid,),
            in_specs=specs,
            out_specs=[pl.BlockSpec(block, index) for _, block, index in outs],
        ),
        out_shape=[shape for shape, _, _ in outs],
        input_output_aliases=alias,
        compiler_params=room(mib),
        cost_estimate=cost(*work),
    )(place, *arrays)


def row_mask(rows, lanes, per, count, wanted, axis):
    at = lax.broadcasted_iota(jnp.int32, (rows, lanes), axis)
    return lax.rem(lax.div(at, jnp.int32(per)), jnp.int32(count)) == wanted


def spread_rows(kept, nbr, per):
    kept = kept.astype(F32)
    return jnp.concatenate(
        [jnp.where(row_mask(*kept.shape, per, nbr, a, 0), kept, 0.0) for a in range(nbr)], axis=1
    ).astype(BF)


def spread_cols(basis, nbr, per):
    basis = basis.astype(F32)
    return jnp.concatenate(
        [jnp.where(row_mask(*basis.shape, per, nbr, a, 1), basis, 0.0) for a in range(nbr)], axis=0
    ).astype(BF)


def widen(coef, blocks):
    return jnp.concatenate(
        [jnp.where(row_mask(*coef.shape, 2, blocks, q, 0), coef, 0.0) for q in range(blocks)],
        axis=1,
    )


def narrow(wide, blocks):
    rows = wide.shape[0]
    return functools.reduce(
        jnp.add,
        [
            jnp.where(
                row_mask(rows, BLOCK, 2, blocks, q, 0), wide[:, q * BLOCK : (q + 1) * BLOCK], 0.0
            )
            for q in range(blocks)
        ],
    )


def fold(pair):
    half = pair.shape[0] // 2
    return pair[:half] + pair[half:]


def prep_kernel(place, all_ref, own_ref, cols_ref, rows_ref, dec_ref, own_dec_ref, kept_ref):
    wide = cols_ref.shape[1]

    def one_hot(picks):
        at = lax.broadcasted_iota(jnp.int32, (wide, picks.shape[-1]), 0)
        return (at == picks).astype(F32).astype(BF)

    dec_ref[0] = dot(cols_ref[...], one_hot(all_ref[0])).astype(BF)
    own = one_hot(own_ref[0])
    own_dec_ref[0] = dot(cols_ref[...], own).astype(BF)
    part = own.shape[1] // 3 * 2
    kept_ref[0] = lax.dot_general(
        own[:, :part], rows_ref[...], (((0,), (0,)), ((), ())), preferred_element_type=F32
    ).astype(BF)


def prep(place, picks_all, picks_own):
    tiles, _, width = picks_all.shape
    own = picks_own.shape[2]
    part = own // 3 * 2
    table = dct_table(BLOCK)
    high = np.asarray(table.astype(BF))
    low = np.asarray((table - high.astype(np.float32)).astype(BF))
    rows = jnp.asarray(np.concatenate([high, low], axis=0))
    cols = jnp.asarray(np.ascontiguousarray(np.concatenate([high, low], axis=0).T))
    each = lambda q, p: (q, 0, 0)
    once = lambda q, p: (0, 0)
    return call(
        prep_kernel,
        tiles,
        [
            (picks_all, (1, 1, width), each),
            (picks_own, (1, 1, own), each),
            (cols, cols.shape, once),
            (rows, rows.shape, once),
        ],
        [
            (shaped((tiles, BLOCK, width), BF), (1, BLOCK, width), each),
            (shaped((tiles, BLOCK, own), BF), (1, BLOCK, own), each),
            (shaped((tiles, part, BLOCK), BF), (1, part, BLOCK), each),
        ],
        4,
        (2 * tiles * 256 * 128 * (width + 2 * own), 2 << 20),
        place,
    )


def project_kernel(nbr, per, place, kept_ref, x_ref, out_ref, xt_ref):
    tiles = kept_ref.shape[0]
    xt_ref[...] = x_ref[0].T
    left = jnp.concatenate([spread_rows(kept_ref[q], nbr, per) for q in range(tiles)], axis=0)
    both = dot(left, xt_ref[...])
    pair = kept_ref.shape[1]
    for q in range(tiles):
        value = fold(both[q * pair : (q + 1) * pair])
        high = value.astype(BF)
        out_ref[q] = jnp.concatenate(
            [high.astype(F32), value - high.astype(F32)], axis=0
        ).astype(BF)


def project(place, kept, acts, step, nbr, per):
    tiles, pair, _ = kept.shape
    _, tokens, rows = acts.shape
    return call(
        functools.partial(project_kernel, nbr, per),
        1,
        [
            (kept, kept.shape, lambda j, p: (0, 0, 0)),
            (acts, (1, tokens, rows), lambda j, p: (step, 0, 0)),
        ],
        [
            (shaped((tiles, pair, tokens), BF), (tiles, pair, tokens), lambda j, p: (0, 0, 0)),
            (shaped((rows, tokens), BF), (rows, tokens), lambda j, p: (0, 0)),
        ],
        14,
        (2 * tiles * pair * rows * tokens, 4 * rows * tokens),
        place,
    )


def keep_rows(kept, moment, nbr, per, blocks):
    return narrow(fold(dot(spread_rows(kept, nbr, per), moment.astype(BF))), blocks)


def natural(position, tiles, place):
    return (mask_at(position // CORES, tiles // CORES) * CORES + position % CORES) ^ place[0]


def moment_rows_kernel(nbr, per, place, kept_ref, m_ref, out_ref):
    out_ref[0] = keep_rows(kept_ref[0], m_ref[0], nbr, per, m_ref.shape[2] // BLOCK)


def moment_rows(place, kept, momentum, tile, per):
    tiles, pair, _ = kept.shape
    rows = momentum.shape[1]
    return call(
        functools.partial(moment_rows_kernel, rows // BLOCK, per),
        tiles,
        [
            (kept, (1, pair, BLOCK), lambda j, p: (j, 0, 0)),
            (momentum, (1, rows, tile), lambda j, p: (0, 0, natural(j, tiles, p))),
        ],
        [(shaped((tiles, pair // 2, BLOCK), F32), (1, pair // 2, BLOCK), lambda j, p: (j, 0, 0))],
        8,
        (2 * tiles * pair * rows * tile, 4 * rows * tile * tiles),
        place,
    )[0]


def error_kernel(place, total_ref, goal_ref, *refs):
    *found, out_ref = refs
    total = total_ref[...] - goal_ref[0].astype(F32)
    for ref in found:
        total = total + ref[...].astype(F32)
    out_ref[...] = total.astype(BF)


def error_of(place, total, found, targets, step):
    shape = total.shape
    whole = lambda j, p: (0, 0)
    return call(
        error_kernel,
        1,
        [(total, shape, whole), (targets, (1,) + shape, lambda j, p: (step, 0, 0))]
        + [(piece, shape, whole) for piece in found],
        [(shaped(shape, BF), shape, whole)],
        6,
        (4 * total.size, 12 * total.size),
        place,
    )[0]


def coef_kernel(scale, place, proj_ref, old_ref, *refs):
    *e_refs, exact_ref, sent_ref = refs
    blocks = e_refs[0].shape[1] // BLOCK
    for q, e_ref in enumerate(e_refs):
        value = 0.9 * old_ref[q] + scale * narrow(fold(dot(proj_ref[q], e_ref[...])), blocks)
        exact_ref[q] = value
        sent_ref[q] = value.astype(BF)


def coefficients(place, proj, errors, old, position):
    tiles = len(errors)
    tokens, tile = errors[0].shape
    pair = proj.shape[1]
    shape = (tiles, pair // 2, BLOCK)
    at = lambda j, p: (position, 0, 0)
    whole = lambda j, p: (0, 0, 0)
    return call(
        functools.partial(coef_kernel, 1.0 / tokens),
        1,
        [(proj, (tiles, pair, tokens), at), (old, shape, at)]
        + [(piece, piece.shape, lambda j, p: (0, 0)) for piece in errors],
        [(shaped(shape, F32), shape, whole), (shaped(shape, BF), shape, whole)],
        8,
        (2 * tiles * pair * tokens * tile, 2 * tiles * tokens * tile),
        place,
    )


def momentum_kernel(scale, nbr, per, follow, place, xt_ref, e_ref, m_ref, dec_ref, coef_ref, *refs):
    refs = list(refs)
    kept_ref = refs.pop(0) if follow else None
    if len(refs) == 2 and not follow:
        refs.pop(0)
    coef = widen(coef_ref[0], m_ref.shape[2] // BLOCK)
    high = coef.astype(BF).astype(F32)
    back = jnp.concatenate([high, high, coef - high], axis=0).astype(BF)
    new = 0.9 * m_ref[0] + (
        dot(xt_ref[...], e_ref[0]) * scale - dot(spread_cols(dec_ref[0], nbr, per), back)
    )
    refs[0][0] = new
    if follow:
        refs[1][0] = keep_rows(kept_ref[0], new, nbr, per, new.shape[1] // BLOCK)


def momentum_step(
    place, acts_t, errors, moment, own_dec, coef, per, start, kept_next, total, previous
):
    rows, tokens = acts_t.shape
    tiles, _, tile = errors.shape
    nbr = rows // BLOCK
    follow = kept_next is not None
    each = lambda j, p: (start + j, 0, 0)
    here = lambda j, p: (j, 0, 0)
    columns = lambda j, p: (0, 0, natural(start + j, total // tile, p))
    ins = [
        (acts_t, acts_t.shape, lambda j, p: (0, 0)),
        (errors, (1, tokens, tile), here),
        (moment, (1, rows, tile), columns if moment.shape[0] == 1 else each),
        (own_dec, (1,) + own_dec.shape[1:], each),
        (coef, (1,) + coef.shape[1:], here),
    ]
    outs = []
    if follow:
        ins.append((kept_next, (1,) + kept_next.shape[1:], each))
        outs.append((shaped((tiles, rows, tile), F32), (1, rows, tile), here))
        outs.append((shaped(coef.shape, F32), (1,) + coef.shape[1:], here))
    else:
        outs.append((shaped((1, rows, total), F32), (1, rows, tile), columns))
    return call(
        functools.partial(momentum_kernel, 1.0 / tokens, nbr, per, follow),
        tiles,
        ins,
        outs,
        14,
        (2 * rows * tokens * tile * tiles, 8 * rows * tile * tiles),
        place,
        previous,
    )


def changed(weight, dec_ref, coef_refs, nbr, per):
    blocks = weight.shape[1] // BLOCK
    parts = []
    for coef_ref in coef_refs:
        parts += [widen(coef_ref[0].astype(F32), blocks)] * 2
    change = dot(spread_cols(dec_ref[0], nbr, per), jnp.concatenate(parts, axis=0).astype(BF))
    return (weight.astype(F32) - 0.1 * change).astype(BF)


def first_kernel(chips, start, cores, place, w_ref, x_ref, *refs):
    out_refs, (w_buf, x_buf, sum_ref, sems) = refs[: len(cores)], refs[len(cores) :]
    total, rows, tile = w_buf.shape
    count = total // len(cores)
    step = x_buf.shape[2]
    tiles = [CORES * (start + at) + core for core in cores for at in range(count)]
    copies = []
    for k in range(rows // step):
        span = slice(k * step, (k + 1) * step)
        copies.append([])
        for at, position in enumerate(tiles):
            column = natural(position, CORES * chips, place) * tile
            source = w_ref.at[span, pl.ds(pl.multiple_of(column, tile), tile)]
            target = w_buf.at[at, span, :]
            copies[k].append(pltpu.make_async_copy(source, target, sems.at[k, at]))
        source = x_ref.at[0, :, span]
        copies[k].append(pltpu.make_async_copy(source, x_buf.at[k], sems.at[k, total]))
    for group in copies:
        for copy in group:
            copy.start()
    for k, group in enumerate(copies):
        span = slice(k * step, (k + 1) * step)
        for copy in group:
            copy.wait()
        for at in range(total):
            part = dot(x_buf[k], w_buf[at, span, :])
            if k > 0:
                part = part + sum_ref[at]
            if k < len(copies) - 1:
                sum_ref[at] = part
            else:
                out_refs[at // count][at % count] = part.astype(BF)


def first(place, weight, acts, tile, start, cores, count):
    rows = weight.shape[0]
    tokens = acts.shape[1]
    step = 256
    hbm = pl.BlockSpec(memory_space=pltpu.HBM)
    total = count * len(cores)
    block = (count, tokens, tile)
    return pl.pallas_call(
        functools.partial(first_kernel, weight.shape[1] // tile // CORES, start, cores),
        grid_spec=pltpu.PrefetchScalarGridSpec(
            num_scalar_prefetch=1,
            grid=(1,),
            in_specs=[hbm, hbm],
            out_specs=[pl.BlockSpec(block, lambda j, p: (0, 0, 0)) for _ in cores],
            scratch_shapes=[
                pltpu.VMEM((total, rows, tile), BF),
                pltpu.VMEM((rows // step, tokens, step), BF),
                pltpu.VMEM((total, tokens, tile), F32),
                pltpu.SemaphoreType.DMA((rows // step, total + 1)),
            ],
        ),
        out_shape=[shaped(block, BF) for _ in cores],
        compiler_params=room(52),
        cost_estimate=cost(2 * tokens * rows * tile * total, 2 * rows * (tile * total + tokens)),
        name="first",
    )(place, weight, acts)


def next_kernel(nbr, per, place, w_ref, x_ref, dec_ref, *refs):
    *coef_refs, new_ref, out_ref = refs
    new = changed(w_ref[...], dec_ref, coef_refs, nbr, per)
    new_ref[0] = new
    out_ref[0] = dot(x_ref[0], new).astype(BF)


def forward(place, weight, acts, step, tile, per, start, core, count, basis, coefs, skip):
    rows = weight.shape[0]
    tokens = acts.shape[1]
    at = lambda j: CORES * (start + j) + core
    ins = [
        (weight, (rows, tile), lambda j, p: (0, natural(at(j), weight.shape[1] // tile, p))),
        (acts, (1, tokens, rows), lambda j, p: (step, 0, 0)),
        (basis, (1,) + basis.shape[1:], lambda j, p: (at(j), 0, 0)),
    ]
    for coef in coefs:
        ins.append((coef, (1,) + coef.shape[1:], lambda j, p: (CORES * (skip + j) + core, 0, 0)))
    product = (shaped((count, tokens, tile), BF), (1, tokens, tile), lambda j, p: (j, 0, 0))
    new = (shaped((count, rows, tile), BF), (1, rows, tile), lambda j, p: (j, 0, 0))
    return call(
        functools.partial(next_kernel, rows // BLOCK, per),
        count,
        ins,
        [new, product],
        12,
        (2 * tokens * rows * tile * count, 2 * rows * tile * count + 2 * tokens * rows),
        place,
    )


def finish_kernel(nbr, per, reps, place, keep_ref, send_ref, dec_ref, *refs):
    here = pl.program_id(0) % CORES == 0

    @pl.when(here)
    def _():
        refs[-1][...] = changed(keep_ref[0], dec_ref, refs[:reps], nbr, per)

    @pl.when(jnp.logical_not(here))
    def _():
        refs[-1][...] = changed(send_ref[0], dec_ref, refs[:reps], nbr, per)


def finish(place, keep, send, basis, coefs, per, start, total, previous, skip):
    count, rows, tile = keep.shape
    each = lambda j, p: (j // CORES, 0, 0)
    return call(
        functools.partial(finish_kernel, rows // BLOCK, per, len(coefs)),
        count * CORES,
        [
            (keep, (1, rows, tile), each),
            (send, (1, rows, tile), each),
            (basis, (1,) + basis.shape[1:], lambda j, p: (CORES * start + j, 0, 0)),
        ]
        + [(coef, (1,) + coef.shape[1:], lambda j, p: (CORES * skip + j, 0, 0)) for coef in coefs],
        [
            (
                shaped((rows, total), BF),
                (rows, tile),
                lambda j, p: (0, natural(CORES * start + j, total // tile, p)),
            )
        ],
        12,
        (2 * rows * 256 * tile * count * CORES, 4 * rows * tile * count * CORES),
        place,
        previous,
    )[0]


def by_distance(value, axes, index):
    for place, axis in enumerate(reversed(axes)):
        value = jnp.where((index >> place & 1) == 1, jnp.flip(value, axis), value)
    return value


def pick_tables(indices, step, reps, parts, replica, tp):
    nbr, nbc = indices.shape[2], indices.shape[3]
    per = nbc // parts * 2
    rep_bits, tp_bits = reps.bit_length() - 1, parts.bit_length() - 1
    picks = indices[step].reshape((2,) * rep_bits + (nbr,) + (2,) * tp_bits + (per,))
    picks = by_distance(picks, range(rep_bits), replica)
    picks = by_distance(picks, range(rep_bits + 1, rep_bits + 1 + tp_bits), tp)
    picks = picks.reshape(reps, nbr, parts // CORES // 2, 2, CORES, per)
    picks = picks.transpose(3, 2, 4, 0, 1, 5)
    picks = picks.reshape(parts, reps, nbr * per)
    both = jnp.concatenate([picks, picks + BLOCK], axis=2)
    own = jnp.concatenate([both[:, 0], picks[:, 0]], axis=1)
    return both.reshape(parts, 1, -1), own.reshape(parts, 1, -1), per


def local(reps, parts, inputs, targets, weight, momentum, indices):
    return steps(reps, parts, inputs, targets, weight, momentum, indices)


def steps(reps, parts, inputs, targets, weight, momentum, indices):
    rows, cols = weight.shape
    nbr = rows // BLOCK
    tile = cols // parts
    chips = parts // CORES
    count = chips // 2
    replica = lax.axis_index("rep").astype(jnp.int32)
    tp = lax.axis_index("tp").astype(jnp.int32)
    place = tp[None]

    acts_t, tables, projected = [None] * STEPS, [None] * STEPS, [None] * STEPS
    chunks = (0, 1)
    mask_of = [mask_at(position, chips) for position in range(chips)]
    groups = ((1, count - 1, 0, 1), (count, count, 1, 0), (0, 1, 0, 0))

    def basis_work(picked):
        for step in range(STEPS):
            picks_all, picks_own, per = pick_tables(picked, step, reps, parts, replica, tp)
            tables[step] = prep(place, picks_all, picks_own)
            projected[step], acts_t[step] = project(place, tables[step][2], inputs, step, nbr, per)
        return moment_rows(place, tables[0][2], momentum, tile, per), per

    moment = momentum
    gathered = [None, None]
    weights = [[None, None] for _ in groups]
    final_m = final_w = None
    for step in range(STEPS):
        last = step == STEPS - 1
        found_all = []
        for group, (start, size, chunk, skip) in enumerate(groups):
            found = [None, None]
            if step == 0 and group != 1:
                found[1], found[0] = first(place, weight, inputs, tile, start, (1, 0), size)
            for core in (1, 0):
                if step == 0 and group == 1:
                    (found[core],) = first(
                        place, weight, inputs, tile, start, (core,), size
                    )
                elif step > 0:
                    weights[group][core], found[core] = forward(
                        place,
                        weight,
                        inputs,
                        step,
                        tile,
                        per,
                        start,
                        core,
                        size,
                        tables[step - 1][0],
                        gathered[chunk],
                        skip,
                    )
                if core == 1:
                    other = swap(found[1], "tp", parts, 1)
            sums = [found[0][at].astype(F32) + other[at].astype(F32) for at in range(size)]
            if start == 0:
                total = sums[0]
                continue
            sums = [value.astype(BF) for value in sums]
            if step == 0 and group == 1:
                *sums, late = lax.optimization_barrier((*sums, indices))
                old, per = basis_work(late)
            for at, value in enumerate(sums):
                mask = mask_of[start + at]
                found_all.append(swap(value, "tp", parts, mask * CORES))
        errors = error_of(place, total, found_all, targets, step)
        pairs, exact, sent = [], [], []
        for position, mask in enumerate(mask_of):
            piece = errors
            if mask:
                piece = swap(errors, "tp", parts, mask * CORES)
            pair = [piece, swap(piece, "tp", parts, 1)]
            value, small = coefficients(place, projected[step], pair, old, position)
            pairs += pair
            exact.append(value)
            sent.append(small)
        for chunk in chunks:
            both = jnp.concatenate(sent[chunk * count : (chunk + 1) * count])
            gathered[chunk] = [both] + [swap(both, "rep", reps, mask) for mask in range(1, reps)]
        update = functools.partial(momentum_step, place, acts_t[step])
        if not last:
            moment, old = update(
                jnp.stack(pairs),
                moment,
                tables[step][1],
                jnp.concatenate(exact),
                per,
                0,
                tables[step + 1][2],
                cols,
                None,
            )
        else:
            for start, size in ((0, 1), (1, count - 1), (count, count)):
                (final_m,) = update(
                    jnp.stack(pairs[start * CORES : (start + size) * CORES]),
                    moment,
                    tables[step][1],
                    jnp.concatenate(exact[start : start + size]),
                    per,
                    start * CORES,
                    None,
                    cols,
                    final_m,
                )
    for group in (2, 0, 1):
        start, _, chunk, skip = groups[group]
        final_w = finish(
            place,
            weights[group][0],
            weights[group][1],
            tables[STEPS - 1][0],
            gathered[chunk],
            per,
            start,
            cols,
            final_w,
            skip,
        )
    return (final_w, final_m)


def solution(mesh):
    reps, parts = mesh.shape["rep"], mesh.shape["tp"]
    in_specs = (
        P(None, "rep", "tp"),
        P(None, "rep", "tp"),
        P("tp", None),
        P("rep", "tp", None),
        P(None, None, "tp", None, None),
    )
    out_specs = (P("tp", None), P("rep", "tp", None))
    return jax.shard_map(
        functools.partial(local, reps, parts),
        mesh=mesh,
        in_specs=in_specs,
        out_specs=out_specs,
        check_vma=False,
    )
```
